32 devices in a mesh: groups: 2 (over x), ctx: 16 (over z, y, core).
Axes of the slice: x: 2, y: 2, z: 4, core: 2. Of those that a mesh axis runs over, the one named last changes fastest.
Arguments:
- inputs: bfloat16 [4096, 8192], P(None, ('groups', 'ctx')), parts along dimension 1, may hold values from -4 to 4
- projections: bfloat16 [512, 8192], P(None, ('groups', 'ctx')), parts along dimension 1, may hold values from -7 to 7
- step_sizes: bfloat16 [64, 8192], P(None, ('groups', 'ctx')), parts along dimension 1, may hold values from 0.0019989014 to 0.019897461
- log_rates: float32 [64], replicated, may hold values from -12 to 3
- skip_gain: float32 [64], replicated, may hold values from 0.5 to 1.5
- packing: int32 [32, 256], P(('groups', 'ctx')), parts along dimension 0, may hold values from 0 to 255, as said below
- prompt_sizes: int32 [8], P('groups'), parts along dimension 0, may hold values from 1 to 3072, 4096 in all
Outputs:
- ssd_output: bfloat16 [4096, 8192], P(None, ('groups', 'ctx')), parts along dimension 1
The draws below stay inside these ranges and needn't reach their ends.
There are 2 independent parts, one for each index of `groups`. The reference program is written for one: setup_inputs(seed, part) draws one part's arguments, and reference() takes and returns one part's arrays. A program takes and returns all parts, laid end to end along the dimension named above; an argument that names none is the same for every part. Nothing has to cross between parts.
Inputs may be any that keep to these rules, and one draw needn't show every extreme that they name: `packing`: each row names every one of the loader's 256 tokens once. `prompt_sizes`: the lengths add up to 4096.
All inputs are finite; a program needn't handle non-finite values.
Results may differ from the reference program's by a relative error of at most 0.001.
The reference program's roundings to bfloat16 on the way count: a program that leaves them out, or rounds other values in their place, can miss the bound.
Values may be sent and summed in bfloat16 or wider, within the bound.
A program may use at most 320 MiB of HBM per device.

```python
import math
import jax
import jax.numpy as jnp
import numpy as np
from jax import lax

H = 64
G = 4
P_SIZE = 64
N = 64
BLOCK = 128
NSEQ = 4
TOK_DEV = 256
TOKENS = 4096
SLOT = 16
N_CTX = 16


def make_order(row_key):
    return jax.random.permutation(row_key, TOK_DEV)


def loader_plan(key):
    row_keys = jax.random.split(jax.random.fold_in(key, 7), N_CTX)
    return jax.vmap(make_order)(row_keys).astype(jnp.int32)


def owner_profile(key):
    loader_order = loader_plan(key)
    slot_width = TOK_DEV // N_CTX
    handed = jnp.broadcast_to(jnp.arange(TOK_DEV, dtype=jnp.int32) // slot_width, (N_CTX, TOK_DEV))
    loader_ids = jnp.broadcast_to(jnp.arange(N_CTX, dtype=jnp.int32)[:, None], (N_CTX, TOK_DEV))
    owners = jnp.zeros((N_CTX, TOK_DEV), jnp.int32).at[loader_ids, loader_order].set(handed).reshape(-1)
    phase_shift = jax.random.randint(jax.random.fold_in(key, 3), (), 0, 8)
    shifted = owners + 8 - phase_shift
    offset = shifted % 8
    pair_signs = (2 * jax.random.randint(jax.random.fold_in(key, 5), (N_CTX // 8 + 2,), 0, 2) - 1).astype(jnp.float32)
    polarity = pair_signs[shifted // 8] * jnp.where(offset == 0, 1.0, -1.0)
    loud_mask = offset < 2
    return (loud_mask, polarity)


def draw_jitter(jitter_key, shape_full):
    jitter = jax.random.truncated_normal(jitter_key, -4.0, 4.0, shape_full, jnp.float32)
    return jitter


def draw_packing(key, part):
    return loader_plan(key)


def draw_inputs(key, part):
    loud_mask, polarity = owner_profile(key)
    jitter_key, mean_key, sign_key = jax.random.split(jax.random.fold_in(key, 21), 3)
    jitter = draw_jitter(jitter_key, (H * P_SIZE, TOKENS))
    magnitude = jax.random.uniform(mean_key, (H * P_SIZE,), jnp.float32, 0.5, 1.0)
    channel_sign = (2 * jax.random.randint(sign_key, (H * P_SIZE,), 0, 2) - 1).astype(jnp.float32)
    common_level = (magnitude * channel_sign)[:, None] * polarity[None, :]
    return jnp.where(loud_mask[None, :], common_level + 0.5 * jitter, jitter).astype(jnp.bfloat16)


def draw_projections(key, part):
    loud_mask, polarity = owner_profile(key)
    jitter = draw_jitter(jax.random.fold_in(key, 31), (G * 2 * N, TOKENS))
    common_level = (0.38 / N) ** 0.5
    row_index = jnp.arange(G * 2 * N, dtype=jnp.int32)
    input_rows = (row_index // N % 2 == 0)[:, None]
    loud_cols = loud_mask[None, :]
    input_map = jnp.where(loud_cols, 5.0 * (common_level + 0.15 * jitter), 0.06 * jitter)
    output_map = jnp.where(loud_cols, 0.2 * (common_level + 0.3 * jitter), 5.0 * (common_level + 0.3 * jitter))
    return jnp.where(input_rows, input_map, output_map).astype(jnp.bfloat16)


def draw_log_rates(key, part):
    order_key, slow_key, mid_key, fast_key = jax.random.split(key, 4)
    head_rank = jax.random.permutation(order_key, H)
    fast_count = H // 4
    mid_count = H // 4
    slow_vals = jax.random.uniform(slow_key, (H,), jnp.float32, jnp.log(0.2), jnp.log(2.3)) - jnp.log(0.0078 * TOKENS)
    mid_vals = jax.random.uniform(mid_key, (H,), jnp.float32, jnp.log(0.36), jnp.log(2.3)) - jnp.log(0.0078 * TOK_DEV)
    fast_vals = jax.random.uniform(fast_key, (H,), jnp.float32, jnp.log(3.0), jnp.log(12.0))
    picked = jnp.where(head_rank < fast_count, fast_vals, jnp.where(head_rank < fast_count + mid_count, mid_vals, slow_vals))
    return picked.astype(jnp.float32)


def block_levels(rng, dims, cuts, least, top_value):
    def one(dim, shards_of):
        steps = jax.random.uniform(jax.random.fold_in(jax.random.fold_in(rng, 6), dim), (shards_of,), jnp.float32, least / len(cuts), top_value / len(cuts))
        return jnp.repeat(jnp.exp(steps), dims[dim] // shards_of).reshape((-1,) + (1,) * (len(dims) - dim - 1))

    loudness = one(*cuts[0])
    for cut in cuts[1:]:
        loudness = loudness * one(*cut)
    return loudness


def length_profile(amount, total, bound, skew):
    weights = [(1 << 20) // math.isqrt(rank ** skew) + 1 for rank in range(2, amount + 1)]
    rest, counts = total - bound - (amount - 1), [1] * (amount - 1)
    while rest > 0:
        movable = [i for i in range(amount - 1) if counts[i] < bound]
        pool, budget = sum([weights[i] for i in movable]), rest
        for i in movable:
            extra = min(bound - counts[i], max(1, budget * weights[i] // pool), rest)
            counts[i] = counts[i] + extra
            rest = rest - extra
    return np.array([bound] + counts)


def ragged_sizes(own_key, count, total, most, lean):
    if count == 2:
        one = jax.random.randint(own_key, (), max(1, total - most), min(most, total - 1) + 1)
        return jnp.stack([one, total - one])
    lengths = jnp.asarray(length_profile(count, total, most, lean), jnp.int32)
    pairs = (count - 1) // 2
    donor, sink = lengths[1:1 + 2 * pairs:2], lengths[2:2 + 2 * pairs:2]
    slack = jnp.minimum(donor - 1, most - sink)
    moved = jax.random.randint(jax.random.fold_in(own_key, 1), (pairs,), 0, 1 << 20) % (slack + 1)
    lengths = lengths.at[1:1 + 2 * pairs:2].set(donor - moved).at[2:2 + 2 * pairs:2].set(sink + moved)
    return lengths[jax.random.permutation(jax.random.fold_in(own_key, 2), count)]


def setup_inputs(seed: int = 0, part: int = 0) -> dict:
    keys = jax.random.split(jax.random.key(seed), 8)
    part_keys = jax.random.split(jax.random.fold_in(keys[7], part), 8)
    return {
        "inputs": draw_inputs(jax.random.fold_in(jax.random.fold_in(keys[7], part), 71), part),
        "projections": draw_projections(jax.random.fold_in(jax.random.fold_in(keys[7], part), 71), part),
        "step_sizes": jnp.clip(jnp.exp(math.log(0.019897461) - 2.2979944 * jax.random.uniform(part_keys[2], (H, TOKENS), jnp.float32) ** block_levels(part_keys[2], (H, TOKENS), ((1, 16),), -0.2, 0.2)), 0.0019989014, 0.019897461).astype(jnp.bfloat16),
        "log_rates": draw_log_rates(jax.random.fold_in(keys[7], 71), part),
        "skip_gain": jnp.clip(jax.random.uniform(keys[4], (H,), jnp.float32, 0.5, 1.5), 0.5, 1.5),
        "packing": draw_packing(jax.random.fold_in(jax.random.fold_in(keys[7], part), 71), part),
        "prompt_sizes": ragged_sizes(part_keys[6], NSEQ, TOKENS, TOKENS * 3 // 4, 2).astype(jnp.int32),
    }


def rounded(value):
    return lax.optimization_barrier(value.astype(jnp.bfloat16)).astype(jnp.float32)


def block_result(block_x, block_bc, block_dt, segment, resets, decay_rate, skip_gain, carry_in):
    length = block_x.shape[1]
    per_group = H // G
    exact = lax.Precision.HIGHEST
    x_heads = block_x.astype(jnp.float32).reshape(G, per_group, P_SIZE, length)
    maps = block_bc.astype(jnp.float32).reshape(G, 2, N, length)
    input_map = maps[:, 0]
    output_map = maps[:, 1]
    step_size = block_dt.astype(jnp.float32)
    log_decay = jnp.cumsum(step_size * decay_rate[:, None], axis=1)
    before_reset = jnp.cumsum(resets) == 0
    column_index = jnp.arange(length, dtype=jnp.int32)
    allowed = (column_index[:, None] >= column_index[None, :]) & (segment[:, None] == segment[None, :])
    decay_gap = log_decay[:, :, None] - log_decay[:, None, :]
    decay_mask = jnp.exp(jnp.where(allowed[None], decay_gap, -jnp.inf))
    scaled_mask = (decay_mask * step_size[:, None, :]).reshape(G, per_group, length, length)
    inner_gram = jnp.einsum("gni,gnj->gij", output_map, input_map, precision=exact)
    mixing = rounded(inner_gram[:, None] * scaled_mask)
    within = jnp.einsum("ghij,ghpj->ghpi", mixing, x_heads, precision=exact)
    opened = jnp.where(before_reset[None, :], jnp.exp(log_decay), jnp.float32(0.0)).reshape(G, per_group, 1, length)
    carried = jnp.einsum("ghpn,gni->ghpi", rounded(carry_in).reshape(G, per_group, P_SIZE, N), output_map, precision=exact)
    result = within + carried * opened + skip_gain.reshape(G, per_group, 1, 1) * x_heads
    last_decay = log_decay[:, -1:]
    into_end = jnp.where((segment == segment[-1])[None, :], jnp.exp(last_decay - log_decay), jnp.float32(0.0)) * step_size
    weighted = rounded(x_heads * into_end.reshape(G, per_group, 1, length))
    block_total = jnp.einsum("ghpj,gnj->ghpn", weighted, input_map, precision=exact).reshape(H, P_SIZE, N)
    block_keep = jnp.where(before_reset[-1], jnp.exp(last_decay[:, 0]), jnp.float32(0.0))
    next_state = block_keep[:, None, None] * carry_in + block_total
    return next_state, result.reshape(-1, length).astype(jnp.bfloat16)


def reference(inputs, projections, step_sizes, log_rates, skip_gain, packing, prompt_sizes):
    loader_base = (jnp.arange(N_CTX, dtype=jnp.int32) * TOK_DEV)[:, None, None]
    source = (packing.reshape(N_CTX, N_CTX, SLOT) + loader_base).transpose(1, 0, 2).reshape(-1).astype(jnp.int32)
    ordered_x = jnp.take(inputs, source, axis=1)
    ordered_bc = jnp.take(projections, source, axis=1)
    ordered_dt = jnp.take(step_sizes, source, axis=1)
    prompt_start = (jnp.cumsum(prompt_sizes) - prompt_sizes).astype(jnp.int32)
    decay_rate = -jnp.exp(log_rates)

    def advance(carry_in, first_col):
        position = first_col + jnp.arange(BLOCK, dtype=jnp.int32)
        segment = jnp.sum((position[:, None] >= prompt_start[None, :]).astype(jnp.int32), axis=1) - 1
        resets = jnp.sum((position[:, None] == prompt_start[None, :]).astype(jnp.int32), axis=1)
        block_x = lax.dynamic_slice_in_dim(ordered_x, first_col, BLOCK, 1)
        block_bc = lax.dynamic_slice_in_dim(ordered_bc, first_col, BLOCK, 1)
        block_dt = lax.dynamic_slice_in_dim(ordered_dt, first_col, BLOCK, 1)
        return block_result(block_x, block_bc, block_dt, segment, resets, decay_rate, skip_gain, carry_in)

    first_cols = jnp.arange(TOKENS // BLOCK, dtype=jnp.int32) * BLOCK
    zero_state = jnp.zeros((H, P_SIZE, N), jnp.float32)
    final_state, blocks_out = lax.scan(advance, zero_state, first_cols)
    return blocks_out.transpose(1, 0, 2).reshape(H * P_SIZE, TOKENS)
```

```python
import functools
import jax
import jax.numpy as jnp
from jax import lax
from jax.experimental import pallas as pl
from jax.experimental.pallas import tpu as pltpu
from jax.sharding import PartitionSpec as P

G = 4
BLOCK = 128
LANES = 128
PLANE = 4
VLIM = 60 * 1024 * 1024
F32 = jnp.float32
BF16 = jnp.bfloat16
MESH = pl.DeviceIdType.MESH


def dot_nt(a, b):
    return lax.dot_general(a, b, (((1,), (1,)), ((), ())), preferred_element_type=F32)


def prep_kernel(pack_ref, x_ref, bc_ref, dt_ref, y_ref, d_ref):
    tok = x_ref.shape[1]
    rows = lax.broadcasted_iota(jnp.int32, (tok, tok), 0)
    pick = jnp.where(rows == pack_ref[...], 1.0, 0.0).astype(F32)
    pick_t = pick.T.astype(BF16)
    wx = x_ref.shape[0]
    y_ref[:, :wx] = dot_nt(pick_t, x_ref[...]).astype(BF16)
    y_ref[:, wx:] = dot_nt(pick_t, bc_ref[...]).astype(BF16)

    @pl.when(pl.program_id(0) == 0)
    def _():
        dt = dot_nt(pick_t, dt_ref[...]).astype(BF16)
        d_ref[...] = jnp.concatenate(
            [dt, jnp.zeros((tok, d_ref.shape[1] - dt.shape[1]), BF16)], axis=1
        )


def exchange_kernel(n, y_ref, d_ref, yo_ref, do_ref, ssem, rsem, lsem):
    me = lax.axis_index("ctx")
    barrier = pltpu.get_barrier_semaphore()

    def greet(off, _):
        pl.semaphore_signal(
            barrier, inc=1, device_id={"ctx": lax.rem(me + off, n)}, device_id_type=MESH
        )
        return 0

    lax.fori_loop(1, n, greet, 0)
    own_y = pltpu.make_async_copy(y_ref.at[me], yo_ref.at[me], lsem.at[0])
    own_d = pltpu.make_async_copy(d_ref.at[me], do_ref.at[me], lsem.at[1])
    own_y.start()
    own_d.start()
    pl.semaphore_wait(barrier, n - 1)

    def copies(off):
        to = lax.rem(me + off, n)
        frm = me
        y = pltpu.make_async_remote_copy(
            y_ref.at[to], yo_ref.at[frm], ssem.at[0, off], rsem.at[0, off],
            device_id={"ctx": to}, device_id_type=MESH)
        d = pltpu.make_async_remote_copy(
            d_ref.at[to], do_ref.at[frm], ssem.at[1, off], rsem.at[1, off],
            device_id={"ctx": to}, device_id_type=MESH)
        return y, d

    half = n // 2

    def start_d(off, _):
        copies(off)[1].start()
        return 0

    def start_pair(i, _):
        copies(half - i)[0].start()

        @pl.when(i > 0)
        def _():
            copies(half + i)[0].start()

        return 0

    lax.fori_loop(1, n, start_d, 0)
    lax.fori_loop(0, half, start_pair, 0)

    def finish(off, _):
        y, d = copies(off)
        d.wait()
        y.wait()
        return 0

    lax.fori_loop(1, n, finish, 0)
    own_y.wait()
    own_d.wait()


def starts_of(sizes_ref):
    out = []
    at = jnp.int32(0)
    for s in range(sizes_ref.shape[0]):
        out.append(at)
        at = at + sizes_ref[s]
    return out


def segment_of(position, starts):
    seg = jnp.zeros(position.shape, jnp.int32)
    for at in starts:
        seg = seg + (position >= at).astype(jnp.int32)
    return seg


def decay_of(dt, rate):
    t = dt.shape[0]
    tri = jnp.where(
        lax.broadcasted_iota(jnp.int32, (t, t), 0) >= lax.broadcasted_iota(jnp.int32, (t, t), 1),
        1.0, 0.0).astype(F32)
    return jnp.dot(tri, dt * rate, preferred_element_type=F32, precision=lax.Precision.HIGHEST)


def spread(value, heads, width):
    rows = value.shape[0]
    per = LANES // width
    lane = lax.broadcasted_iota(jnp.int32, (rows, LANES), 1)
    out = []
    for q in range(heads // per):
        acc = jnp.broadcast_to(value[:, q * per:q * per + 1], (rows, LANES))
        for k in range(1, per):
            other = jnp.broadcast_to(value[:, q * per + k:q * per + k + 1], (rows, LANES))
            acc = jnp.where(lane >= k * width, other, acc)
        out.append(acc)
    return jnp.concatenate(out, axis=1)


def group_lanes(value, g, per_group):
    return pltpu.roll(value, lax.rem(LANES - g * per_group, LANES), 1)


def states_kernel(heads, width, states, sizes_ref, rate_ref, y_ref, d_ref, t_ref, t0_ref):
    g = pl.program_id(0)
    tok = y_ref.shape[0]
    wx = heads * width
    starts = starts_of(sizes_ref)
    base = lax.axis_index("ctx") * tok
    rate = group_lanes(-jnp.exp(rate_ref[...]), g, heads)[0:1]
    total = None
    for b in range(tok // BLOCK):
        lo = b * BLOCK
        first = base + lo
        last = first + BLOCK - 1
        dt = group_lanes(d_ref[lo:lo + BLOCK, :].astype(F32), g, heads)
        cum = decay_of(dt, rate)
        end = cum[BLOCK - 1:BLOCK, :]
        pos = first + lax.broadcasted_iota(jnp.int32, (BLOCK, LANES), 0)
        last_seg = jnp.int32(0)
        cut = jnp.int32(0)
        for at in starts:
            last_seg = last_seg + (last >= at).astype(jnp.int32)
            cut = cut + ((at >= first) & (at <= last)).astype(jnp.int32)
        same = segment_of(pos, starts) == last_seg
        into = jnp.where(same, jnp.exp(end - cum), 0.0) * dt
        weighted = (y_ref[lo:lo + BLOCK, :wx].astype(F32) * spread(into, heads, width)).astype(BF16)
        maps_t = y_ref[lo:lo + BLOCK, wx:].astype(F32).T
        in_map = maps_t[:states].astype(BF16)
        block_total = jnp.dot(in_map, weighted, preferred_element_type=F32)
        keep_h = jnp.where(cut == 0, jnp.exp(end), 0.0)
        keep = spread(jnp.broadcast_to(keep_h, (8, LANES)), heads, width)
        if total is None:
            total, gain = block_total, keep
        else:
            total = keep[0:1] * total + block_total
            gain = gain * keep
        if b < tok // BLOCK - 1:
            t0_ref[b, :states, :] = block_total
            t0_ref[b, states:, :] = keep
    t_ref[:states, :] = total
    t_ref[states:, :] = gain


def chain_kernel(n, states, chunks, t_ref, c_ref, early, first, chip, enter, leave, ssem, rsem):
    me = lax.axis_index("ctx")
    q = lax.rem(me, PLANE)
    z = me // PLANE
    nz = n // PLANE
    cw = t_ref.shape[1] // chunks
    barrier = pltpu.get_barrier_semaphore()

    def hail(to):
        pl.semaphore_signal(barrier, inc=1, device_id={"ctx": to}, device_id_type=MESH)

    @pl.when(q == 0)
    def _():
        hail(me + 1)
        pl.semaphore_wait(barrier, 1)

    @pl.when(q == 1)
    def _():
        hail(me - 1)
        hail(me + 2)
        pl.semaphore_wait(barrier, 2)

    @pl.when(q == 2)
    def _():
        hail(me + 1)
        pl.semaphore_wait(barrier, 1)

    @pl.when(q == 3)
    def _():
        hail(me - 1)
        hail(me - 2)

        @pl.when(z > 0)
        def _():
            hail(me - PLANE)

        @pl.when(z < nz - 1)
        def _():
            hail(me + PLANE)

        pl.semaphore_wait(barrier, 2 + jnp.where(z > 0, 1, 0) + jnp.where(z < nz - 1, 1, 0))

    def sl(ref, c):
        return ref.at[:, pl.ds(pl.multiple_of(c * cw, LANES), cw)]

    def push(kind, way, c, src, dst, to):
        return pltpu.make_async_remote_copy(
            sl(src, c), sl(dst, c), ssem.at[way, c], rsem.at[kind, c],
            device_id={"ctx": to}, device_id_type=MESH)

    EARLY, FIRST, ENTER = 0, 1, 2

    def lanes(c):
        return pl.ds(pl.multiple_of(c * cw, LANES), cw)

    def join(old, new):
        gain = new[states:states + 1]
        return jnp.concatenate([gain * old[:states] + new[:states], old[states:] * new[states:]], axis=0)

    def loop(body):
        def step(c, _):
            body(c)
            return 0
        lax.fori_loop(0, chunks, step, 0)

    @pl.when(q == 0)
    def _():
        loop(lambda c: push(EARLY, 0, c, t_ref, early, me + 1).start())

        def body(c):
            s = lanes(c)

            @pl.when(z > 0)
            def _():
                push(ENTER, 1, c, enter, enter, me + 1).wait_recv()
                c_ref[:, s] = enter[:, s]

            @pl.when(z == 0)
            def _():
                c_ref[:, s] = jnp.zeros((states, cw), F32)

        loop(body)
        loop(lambda c: push(EARLY, 0, c, t_ref, early, me + 1).wait_send())

    @pl.when(q == 1)
    def _():
        def up(c):
            s = lanes(c)
            push(EARLY, 0, c, t_ref, early, me - 1).wait_recv()
            chip[:, s] = join(early[:, s], t_ref[:, s])
            push(FIRST, 0, c, chip, first, me + 2).start()

        loop(up)

        def body(c):
            s = lanes(c)

            @pl.when(z > 0)
            def _():
                push(ENTER, 1, c, enter, enter, me - 1).wait_recv()
                push(ENTER, 1, c, enter, enter, me - 1).start()
                c_ref[:, s] = early[states:states + 1, s] * enter[:, s] + early[:states, s]

            @pl.when(z == 0)
            def _():
                c_ref[:, s] = early[:states, s]

        loop(body)
        loop(lambda c: push(FIRST, 0, c, chip, first, me + 2).wait_send())

        @pl.when(z > 0)
        def _():
            loop(lambda c: push(ENTER, 1, c, enter, enter, me - 1).wait_send())

    @pl.when(q == 2)
    def _():
        loop(lambda c: push(EARLY, 0, c, t_ref, early, me + 1).start())

        def body(c):
            s = lanes(c)
            push(FIRST, 1, c, first, first, me + 1).wait_recv()

            @pl.when(z > 0)
            def _():
                push(ENTER, 1, c, enter, enter, me + 1).wait_recv()
                c_ref[:, s] = first[states:states + 1, s] * enter[:, s] + first[:states, s]

            @pl.when(z == 0)
            def _():
                c_ref[:, s] = first[:states, s]

        loop(body)
        loop(lambda c: push(EARLY, 0, c, t_ref, early, me + 1).wait_send())

    @pl.when(q == 3)
    def _():
        def body(c):
            s = lanes(c)
            push(EARLY, 0, c, t_ref, early, me - 1).wait_recv()
            push(FIRST, 0, c, first, first, me - 1).wait_recv()
            push(FIRST, 0, c, first, first, me - 1).start()
            mine = join(first[:, s], early[:, s])
            whole = join(mine, t_ref[:, s])

            @pl.when(z > 0)
            def _():
                push(ENTER, 1, c, enter, enter, me - 1).wait_recv()
                came = enter[:, s]

                @pl.when(z < nz - 1)
                def _():
                    leave[:, s] = whole[states:states + 1] * came + whole[:states]
                    push(ENTER, 3, c, leave, enter, me + PLANE).start()

                push(ENTER, 2, c, enter, enter, me - 2).start()
                push(ENTER, 1, c, enter, enter, me - 1).start()
                c_ref[:, s] = mine[states:states + 1] * came + mine[:states]

            @pl.when(z == 0)
            def _():
                @pl.when(z < nz - 1)
                def _():
                    leave[:, s] = whole[:states]
                    push(ENTER, 3, c, leave, enter, me + PLANE).start()

                c_ref[:, s] = mine[:states]

        loop(body)
        loop(lambda c: push(FIRST, 0, c, first, first, me - 1).wait_send())

        @pl.when(z < nz - 1)
        def _():
            loop(lambda c: push(ENTER, 3, c, leave, enter, me + PLANE).wait_send())

        @pl.when(z > 0)
        def _():
            loop(lambda c: push(ENTER, 2, c, enter, enter, me - 2).wait_send())
            loop(lambda c: push(ENTER, 1, c, enter, enter, me - 1).wait_send())


def output_kernel(heads, width, states, sizes_ref, skip_ref, rate_ref, y_ref, d_ref, c_ref, t0_ref, o_ref):
    g = pl.program_id(0)
    tok = y_ref.shape[0]
    wx = heads * width
    starts = starts_of(sizes_ref)
    base = lax.axis_index("ctx") * tok
    rate = group_lanes(-jnp.exp(rate_ref[...]), g, heads)[0:1]
    carry = c_ref[...]
    for b in range(tok // BLOCK):
        lo = b * BLOCK
        first = base + lo
        dt = group_lanes(d_ref[lo:lo + BLOCK, :].astype(F32), g, heads)
        cum = decay_of(dt, rate)
        cum_t = cum.T
        dt_t = dt.T
        pos_i = first + lax.broadcasted_iota(jnp.int32, (BLOCK, BLOCK), 0)
        pos_j = first + lax.broadcasted_iota(jnp.int32, (BLOCK, BLOCK), 1)
        allowed = (pos_i >= pos_j) & (segment_of(pos_i, starts) == segment_of(pos_j, starts))
        row_pos = first + lax.broadcasted_iota(jnp.int32, (1, BLOCK), 1)
        cut = jnp.zeros((1, BLOCK), jnp.int32)
        for at in starts:
            cut = cut + ((row_pos >= at) & (at >= first)).astype(jnp.int32)
        opened = jnp.where(cut == 0, jnp.exp(cum_t[:heads]), 0.0)
        maps = y_ref[lo:lo + BLOCK, wx:]
        in_map = maps[:, :states]
        out_map = maps[:, states:]
        gram = dot_nt(out_map, in_map)
        x_fm = y_ref[lo:lo + BLOCK, :wx].T
        carried = dot_nt(carry.astype(BF16).T, out_map)
        for h in range(heads):
            gap = jnp.broadcast_to(cum[:, h:h + 1], (BLOCK, BLOCK)) - cum_t[h:h + 1]
            mask = jnp.exp(jnp.where(allowed, gap, -jnp.inf))
            mixing = (gram * (mask * dt_t[h:h + 1])).astype(BF16)
            r = slice(h * width, (h + 1) * width)
            xh = x_fm[r]
            res = dot_nt(xh, mixing) + carried[r] * opened[h:h + 1]
            res = res + skip_ref[g * heads + h] * xh.astype(F32)
            o_ref[r, lo:lo + BLOCK] = res.astype(BF16)
        if b < tok // BLOCK - 1:
            carry = t0_ref[b, states:states + 1, :] * carry + t0_ref[b, :states, :]


def per_device(n, inputs, projections, step_sizes, log_rates, skip_gain, packing, prompt_sizes):
    tok = inputs.shape[1]
    head_count = log_rates.shape[0]
    heads = head_count // G
    states = projections.shape[0] // (2 * G)
    width = inputs.shape[0] // head_count
    wx = heads * width
    wm = 2 * states
    slot = tok // n
    vmem = pl.BlockSpec(memory_space=pltpu.VMEM)
    smem = pl.BlockSpec(memory_space=pltpu.SMEM)
    sds = jax.ShapeDtypeStruct
    y, d = pl.pallas_call(
        prep_kernel,
        grid=(G,),
        in_specs=[
            pl.BlockSpec((1, tok), lambda g: (0, 0)),
            pl.BlockSpec((wx, tok), lambda g: (g, 0)),
            pl.BlockSpec((wm, tok), lambda g: (g, 0)),
            pl.BlockSpec((head_count, tok), lambda g: (0, 0)),
        ],
        out_specs=[
            pl.BlockSpec((tok, wx + wm), lambda g: (0, g)),
            pl.BlockSpec((tok, LANES), lambda g: (0, 0)),
        ],
        out_shape=[sds((tok, G * (wx + wm)), BF16), sds((tok, LANES), BF16)],
        name="prep",
    )(packing, inputs, projections, step_sizes)
    y = y.reshape(n, slot, G * (wx + wm))
    d = d.reshape(n, slot, LANES)
    y, d = pl.pallas_call(
        functools.partial(exchange_kernel, n),
        in_specs=[vmem, vmem],
        out_specs=[vmem, vmem],
        out_shape=[sds(y.shape, BF16), sds(d.shape, BF16)],
        scratch_shapes=[
            pltpu.SemaphoreType.DMA((2, n)),
            pltpu.SemaphoreType.DMA((2, n)),
            pltpu.SemaphoreType.DMA((2,)),
        ],
        compiler_params=pltpu.CompilerParams(collective_id=0, has_side_effects=True, vmem_limit_bytes=VLIM),
        name="exchange",
    )(y, d)
    y = y.reshape(tok, G * (wx + wm))
    d = d.reshape(tok, LANES)
    rates = jnp.pad(log_rates, (0, LANES - head_count)).reshape(1, LANES)
    rates = jnp.broadcast_to(rates, (8, LANES))
    blocks = tok // BLOCK
    rows = states + 8
    y_spec = pl.BlockSpec((tok, wx + wm), lambda g: (0, g))
    d_spec = pl.BlockSpec((tok, LANES), lambda g: (0, 0))
    r_spec = pl.BlockSpec((8, LANES), lambda g: (0, 0))
    t0_spec = pl.BlockSpec((blocks - 1, rows, wx), lambda g: (0, 0, g))
    t, t0 = pl.pallas_call(
        functools.partial(states_kernel, heads, width, states),
        grid=(G,),
        in_specs=[smem, r_spec, y_spec, d_spec],
        out_specs=[pl.BlockSpec((rows, wx), lambda g: (0, g)), t0_spec],
        out_shape=[sds((rows, G * wx), F32), sds((blocks - 1, rows, G * wx), F32)],
        name="states",
    )(prompt_sizes, rates, y, d)
    chunks = 8
    full = (rows, G * wx)
    only = (states, G * wx)
    carry = pl.pallas_call(
        functools.partial(chain_kernel, n, states, chunks),
        in_specs=[vmem],
        out_specs=vmem,
        out_shape=sds(only, F32),
        scratch_shapes=[
            pltpu.VMEM(full, F32),
            pltpu.VMEM(full, F32),
            pltpu.VMEM(full, F32),
            pltpu.VMEM(only, F32),
            pltpu.VMEM(only, F32),
            pltpu.SemaphoreType.DMA((4, chunks)),
            pltpu.SemaphoreType.DMA((3, chunks)),
        ],
        compiler_params=pltpu.CompilerParams(collective_id=1, has_side_effects=True, vmem_limit_bytes=VLIM),
        name="chain",
    )(t)
    return pl.pallas_call(
        functools.partial(output_kernel, heads, width, states),
        grid=(G,),
        in_specs=[smem, smem, r_spec, y_spec, d_spec,
                  pl.BlockSpec((states, wx), lambda g: (0, g)), t0_spec],
        out_specs=pl.BlockSpec((wx, tok), lambda g: (g, 0)),
        out_shape=sds((G * wx, tok), BF16),
        name="output",
    )(prompt_sizes, skip_gain, rates, y, d, carry, t0)


def solution(mesh):
    in_specs = (
        P(None, ("groups", "ctx")),
        P(None, ("groups", "ctx")),
        P(None, ("groups", "ctx")),
        P(),
        P(),
        P(("groups", "ctx"), None),
        P("groups"),
    )
    out_specs = P(None, ("groups", "ctx"))
    return jax.shard_map(
        functools.partial(per_device, mesh.shape["ctx"]),
        mesh=mesh, in_specs=in_specs, out_specs=out_specs, check_vma=False,
    )
```

```python
import functools
import jax
import jax.numpy as jnp
from jax import lax
from jax.experimental import pallas as pl
from jax.experimental.pallas import tpu as pltpu
from jax.sharding import PartitionSpec as P

G = 4
BLOCK = 128
LANES = 128
PLANE = 4
VLIM = 60 * 1024 * 1024
F32 = jnp.float32
BF16 = jnp.bfloat16
MESH = pl.DeviceIdType.MESH


def dot_nt(a, b):
    return lax.dot_general(a, b, (((1,), (1,)), ((), ())), preferred_element_type=F32)


def starts_of(sizes_ref):
    out = []
    at = jnp.int32(0)
    for s in range(sizes_ref.shape[0]):
        out.append(at)
        at = at + sizes_ref[s]
    return out


def segment_of(position, starts):
    seg = jnp.zeros(position.shape, jnp.int32)
    for at in starts:
        seg = seg + (position >= at).astype(jnp.int32)
    return seg


def decay_of(dt, rate):
    t = dt.shape[0]
    tri = jnp.where(
        lax.broadcasted_iota(jnp.int32, (t, t), 0) >= lax.broadcasted_iota(jnp.int32, (t, t), 1),
        1.0, 0.0).astype(F32)
    return jnp.dot(tri, dt * rate, preferred_element_type=F32, precision=lax.Precision.HIGHEST)


def spread(value, heads, width):
    rows = value.shape[0]
    per = LANES // width
    lane = lax.broadcasted_iota(jnp.int32, (rows, LANES), 1)
    out = []
    for q in range(heads // per):
        acc = jnp.broadcast_to(value[:, q * per:q * per + 1], (rows, LANES))
        for k in range(1, per):
            other = jnp.broadcast_to(value[:, q * per + k:q * per + k + 1], (rows, LANES))
            acc = jnp.where(lane >= k * width, other, acc)
        out.append(acc)
    return jnp.concatenate(out, axis=1)


def group_lanes(value, g, per_group):
    return pltpu.roll(value, lax.rem(LANES - g * per_group, LANES), 1)


def fused_kernel(
    n, heads, width, states, sub,
    sizes_ref, skip_ref, rate_ref, pack_ref, x_hbm, bc_hbm, dt_ref, o_hbm,
    xv, bv, pick, ys, yr, ds, dr, cums, dts, acc, opens, obuf,
    t_ref, t0_ref, early, first, mine, whole, leave, enter, c_ref,
    in_sem, out_sem, own_sem, own_d_sem, xs_sem, xr_sem, dsend_sem, drecv_sem, ssem, rsem,
):
    me = lax.axis_index("ctx")
    tok = dt_ref.shape[1]
    slot = tok // n
    wx = heads * width
    wm = 2 * states
    blocks = tok // BLOCK
    half = n // 2
    q = lax.rem(me, PLANE)
    z = me // PLANE
    nz = n // PLANE
    cw = wx // sub
    starts = starts_of(sizes_ref)
    base = me * tok

    def loop(count, body, low=0):
        def step(i, _):
            body(i)
            return 0
        lax.fori_loop(low, count, step, 0)

    barrier = pltpu.get_barrier_semaphore()
    loop(n, lambda off: pl.semaphore_signal(
        barrier, inc=1, device_id={"ctx": lax.rem(me + off, n)}, device_id_type=MESH), low=1)

    def load(g):
        rx = pl.ds(pl.multiple_of(g * wx, LANES), wx)
        rb = pl.ds(pl.multiple_of(g * wm, LANES), wm)
        return (
            pltpu.make_async_copy(x_hbm.at[rx], xv.at[g], in_sem.at[0, g]),
            pltpu.make_async_copy(bc_hbm.at[rb], bv.at[g], in_sem.at[1, g]),
        )

    def begin(g):
        for part in load(g):
            part.start()

    loop(G, begin)

    rows = lax.broadcasted_iota(jnp.int32, (tok, tok), 0)
    pick[...] = jnp.where(rows == pack_ref[...], 1.0, 0.0).astype(F32).T.astype(BF16)
    head_count = dt_ref.shape[0]
    dt_all = dot_nt(pick[...], dt_ref[...]).astype(BF16)
    dt_all = jnp.concatenate([dt_all, jnp.zeros((tok, LANES - head_count), BF16)], axis=1)
    ds[...] = dt_all.reshape(n, slot, LANES)

    def prep(g):
        for part in load(g):
            part.wait()
        yx = dot_nt(pick[...], xv[g]).astype(BF16)
        yb = dot_nt(pick[...], bv[g]).astype(BF16)
        ys[g, :, :, :wx] = yx.reshape(n, slot, wx)
        ys[g, :, :, wx:] = yb.reshape(n, slot, wm)

    def send_y(g, off):
        to = lax.rem(me + off, n)
        return pltpu.make_async_remote_copy(
            ys.at[g, to], yr.at[g, me], xs_sem.at[g, off], xr_sem.at[g, off],
            device_id={"ctx": to}, device_id_type=MESH)

    def send_d(off):
        to = lax.rem(me + off, n)
        return pltpu.make_async_remote_copy(
            ds.at[to], dr.at[me], dsend_sem.at[off], drecv_sem.at[off],
            device_id={"ctx": to}, device_id_type=MESH)

    def keep_y(g):
        return pltpu.make_async_copy(ys.at[g, me], yr.at[g, me], own_sem.at[g])

    def keep_d():
        return pltpu.make_async_copy(ds.at[me], dr.at[me], own_d_sem.at[0])

    def send_all(g):
        def pair(i):
            send_y(g, half - i).start()

            @pl.when(i > 0)
            def _():
                send_y(g, half + i).start()

        loop(half, pair)
        keep_y(g).start()

    prep(0)
    pl.semaphore_wait(barrier, n - 1)
    loop(n, lambda off: send_d(off).start(), low=1)
    keep_d().start()

    def prep_next(g):
        @pl.when(g < G - 1)
        def _():
            prep(g + 1)
        send_all(g)

    loop(G, prep_next)

    def push(kind, way, g, k, src, dst, to):
        s = pl.ds(pl.multiple_of(k * cw, LANES), cw)
        return pltpu.make_async_remote_copy(
            src.at[g, :, s], dst.at[g, :, s], ssem.at[way, g, k], rsem.at[kind, g, k],
            device_id={"ctx": to}, device_id_type=MESH)

    EARLY, FIRST, ENTER = 0, 1, 2

    def lanes(k):
        return pl.ds(pl.multiple_of(k * cw, LANES), cw)

    def join(old, new):
        gain = new[states:states + 1]
        return jnp.concatenate([gain * old[:states] + new[:states], old[states:] * new[states:]], axis=0)

    def local_stage(g):
        @pl.when((q == 0) | (q == 2))
        def _():
            loop(sub, lambda k: push(EARLY, 0, g, k, t_ref, early, me + 1).start())

        @pl.when(q == 1)
        def _():
            def up(k):
                s = lanes(k)
                push(EARLY, 0, g, k, t_ref, early, me - 1).wait_recv()
                whole[g, :, s] = join(early[g, :, s], t_ref[g, :, s])
                push(FIRST, 0, g, k, whole, first, me + 2).start()
            loop(sub, up)

        @pl.when(q == 3)
        def _():
            def up(k):
                s = lanes(k)
                push(EARLY, 0, g, k, t_ref, early, me - 1).wait_recv()
                push(FIRST, 0, g, k, first, first, me - 1).wait_recv()
                push(FIRST, 0, g, k, first, first, me - 1).start()
                both = join(first[g, :, s], early[g, :, s])
                mine[:, s] = both
                every = join(both, t_ref[g, :, s])
                whole[g, :, s] = every

                @pl.when((z == 0) & (nz > 1))
                def _():
                    leave[g, :, s] = every[:states]
                    push(ENTER, 3, g, k, leave, enter, me + PLANE).start()
            loop(sub, up)

    def carry_stage(g):
        def merge(local, k):
            s = lanes(k)

            @pl.when(z > 0)
            def _():
                c_ref[:, s] = local[states:states + 1] * enter[g, :, s] + local[:states]

            @pl.when(z == 0)
            def _():
                c_ref[:, s] = local[:states]

        @pl.when(q == 0)
        def _():
            def body(k):
                s = lanes(k)

                @pl.when(z > 0)
                def _():
                    push(ENTER, 1, g, k, enter, enter, me + 1).wait_recv()
                    c_ref[:, s] = enter[g, :, s]

                @pl.when(z == 0)
                def _():
                    c_ref[:, s] = jnp.zeros((states, cw), F32)
            loop(sub, body)

        @pl.when(q == 1)
        def _():
            def body(k):
                @pl.when(z > 0)
                def _():
                    push(ENTER, 1, g, k, enter, enter, me - 1).wait_recv()
                    push(ENTER, 1, g, k, enter, enter, me - 1).start()
                merge(early[g, :, lanes(k)], k)
            loop(sub, body)

        @pl.when(q == 2)
        def _():
            def body(k):
                push(FIRST, 1, g, k, first, first, me + 1).wait_recv()

                @pl.when(z > 0)
                def _():
                    push(ENTER, 1, g, k, enter, enter, me + 1).wait_recv()
                merge(first[g, :, lanes(k)], k)
            loop(sub, body)

        @pl.when(q == 3)
        def _():
            def body(k):
                s = lanes(k)

                @pl.when(z > 0)
                def _():
                    push(ENTER, 1, g, k, enter, enter, me - 1).wait_recv()

                    @pl.when(z < nz - 1)
                    def _():
                        leave[g, :, s] = (
                            whole[g, states:states + 1, s] * enter[g, :, s] + whole[g, :states, s])
                        push(ENTER, 3, g, k, leave, enter, me + PLANE).start()

                    push(ENTER, 2, g, k, enter, enter, me - 2).start()
                    push(ENTER, 1, g, k, enter, enter, me - 1).start()
                merge(mine[:, s], k)
            loop(sub, body)

    def settle(g):
        def one(k):
            @pl.when((q == 0) | (q == 2))
            def _():
                push(EARLY, 0, g, k, t_ref, early, me + 1).wait_send()

            @pl.when(q == 1)
            def _():
                push(FIRST, 0, g, k, whole, first, me + 2).wait_send()

                @pl.when(z > 0)
                def _():
                    push(ENTER, 1, g, k, enter, enter, me - 1).wait_send()

            @pl.when(q == 3)
            def _():
                push(FIRST, 0, g, k, first, first, me - 1).wait_send()

                @pl.when(z < nz - 1)
                def _():
                    push(ENTER, 3, g, k, leave, enter, me + PLANE).wait_send()

                @pl.when(z > 0)
                def _():
                    push(ENTER, 2, g, k, enter, enter, me - 2).wait_send()
                    push(ENTER, 1, g, k, enter, enter, me - 1).wait_send()
        loop(sub, one)

    rate_all = jnp.concatenate(
        [rate_ref[...], jnp.zeros((1, LANES - head_count), F32)], axis=1)
    rate_all = jnp.broadcast_to(-jnp.exp(rate_all), (8, LANES))

    def rows_of(b):
        return slice(b * BLOCK // slot, (b + 1) * BLOCK // slot)

    def y_of(g, b, lo, hi):
        return yr[g, rows_of(b), :, lo:hi].reshape(BLOCK, hi - lo)

    def states_stage(g):
        rate = group_lanes(rate_all, g, heads)[0:1]
        total = None
        for b in range(blocks):
            lo = b * BLOCK
            head = base + lo
            last = head + BLOCK - 1
            dt = dr[rows_of(b)].reshape(BLOCK, LANES).astype(F32)
            dt = group_lanes(dt, g, heads)
            cum = decay_of(dt, rate)
            cums[lo:lo + BLOCK, :] = cum
            dts[lo:lo + BLOCK, :] = dt
            end = cum[BLOCK - 1:BLOCK, :]
            pos = head + lax.broadcasted_iota(jnp.int32, (BLOCK, LANES), 0)
            last_seg = jnp.int32(0)
            cut = jnp.int32(0)
            for at in starts:
                last_seg = last_seg + (last >= at).astype(jnp.int32)
                cut = cut + ((at >= head) & (at <= last)).astype(jnp.int32)
            same = segment_of(pos, starts) == last_seg
            into = jnp.where(same, jnp.exp(end - cum), 0.0) * dt
            weighted = (y_of(g, b, 0, wx).astype(F32) * spread(into, heads, width)).astype(BF16)
            maps_t = y_of(g, b, wx, wx + wm).astype(F32).T
            in_map = maps_t[:states].astype(BF16)
            block_total = jnp.dot(in_map, weighted, preferred_element_type=F32)
            keep_h = jnp.where(cut == 0, jnp.exp(end), 0.0)
            keep = spread(jnp.broadcast_to(keep_h, (8, LANES)), heads, width)
            if total is None:
                total, gain = block_total, keep
            else:
                total = keep[0:1] * total + block_total
                gain = gain * keep
            if b < blocks - 1:
                t0_ref[b, :states, :] = block_total
                t0_ref[b, states:, :] = keep
        t_ref[g, :states, :] = total
        t_ref[g, states:, :] = gain

    def inner_stage(g):
        for b in range(blocks):
            lo = b * BLOCK
            head = base + lo
            cum = cums[lo:lo + BLOCK, :]
            cum_t = cum.T
            dt_t = dts[lo:lo + BLOCK, :].T
            pos_i = head + lax.broadcasted_iota(jnp.int32, (BLOCK, BLOCK), 0)
            pos_j = head + lax.broadcasted_iota(jnp.int32, (BLOCK, BLOCK), 1)
            allowed = (pos_i >= pos_j) & (segment_of(pos_i, starts) == segment_of(pos_j, starts))
            row_pos = head + lax.broadcasted_iota(jnp.int32, (1, BLOCK), 1)
            cut = jnp.zeros((1, BLOCK), jnp.int32)
            for at in starts:
                cut = cut + ((row_pos >= at) & (at >= head)).astype(jnp.int32)
            opens[b] = jnp.where(cut == 0, jnp.exp(cum_t[:heads]), 0.0)
            in_map = y_of(g, b, wx, wx + states)
            out_map = y_of(g, b, wx + states, wx + wm)
            gram = dot_nt(out_map, in_map)
            x_fm = y_of(g, b, 0, wx).T
            for h in range(heads):
                gap = jnp.broadcast_to(cum[:, h:h + 1], (BLOCK, BLOCK)) - cum_t[h:h + 1]
                mask = jnp.exp(jnp.where(allowed, gap, -jnp.inf))
                mixing = (gram * (mask * dt_t[h:h + 1])).astype(BF16)
                r = slice(h * width, (h + 1) * width)
                xh = x_fm[r]
                acc[r, lo:lo + BLOCK] = (
                    dot_nt(xh, mixing) + skip_ref[g * heads + h] * xh.astype(F32))

    def store_out(g):
        return pltpu.make_async_copy(
            obuf.at[g], o_hbm.at[pl.ds(pl.multiple_of(g * wx, LANES), wx)], out_sem.at[g])

    def output_stage(g):
        carry = c_ref[...]
        for b in range(blocks):
            lo = b * BLOCK
            out_map = y_of(g, b, wx + states, wx + wm)
            carried = dot_nt(carry.astype(BF16).T, out_map)
            for h in range(heads):
                r = slice(h * width, (h + 1) * width)
                obuf[g, r, lo:lo + BLOCK] = (
                    acc[r, lo:lo + BLOCK] + carried[r] * opens[b, h:h + 1]).astype(BF16)
            if b < blocks - 1:
                carry = t0_ref[b, states:states + 1, :] * carry + t0_ref[b, :states, :]
        store_out(g).start()

    loop(n, lambda off: send_d(off).wait_recv(), low=1)
    keep_d().wait()

    def turn(g):
        loop(n, lambda off: send_y(g, off).wait_recv(), low=1)
        keep_y(g).wait()
        states_stage(g)
        local_stage(g)
        inner_stage(g)
        carry_stage(g)
        output_stage(g)

    loop(G, turn)
    loop(n, lambda off: send_d(off).wait_send(), low=1)

    def close(g):
        loop(n, lambda off: send_y(g, off).wait_send(), low=1)
        settle(g)
        store_out(g).wait()

    loop(G, close)


def per_device(n, inputs, projections, step_sizes, log_rates, skip_gain, packing, prompt_sizes):
    tok = inputs.shape[1]
    head_count = log_rates.shape[0]
    heads = head_count // G
    states = projections.shape[0] // (2 * G)
    width = inputs.shape[0] // head_count
    wx = heads * width
    wm = 2 * states
    slot = tok // n
    blocks = tok // BLOCK
    rows = states + 8
    sub = 4
    vmem = pl.BlockSpec(memory_space=pltpu.VMEM)
    smem = pl.BlockSpec(memory_space=pltpu.SMEM)
    hbm = pl.BlockSpec(memory_space=pl.ANY)
    dma = pltpu.SemaphoreType.DMA
    return pl.pallas_call(
        functools.partial(fused_kernel, n, heads, width, states, sub),
        in_specs=[smem, smem, vmem, vmem, hbm, hbm, vmem],
        out_specs=hbm,
        out_shape=jax.ShapeDtypeStruct((G * wx, tok), BF16),
        scratch_shapes=[
            pltpu.VMEM((G, wx, tok), BF16),
            pltpu.VMEM((G, wm, tok), BF16),
            pltpu.VMEM((tok, tok), BF16),
            pltpu.VMEM((G, n, slot, wx + wm), BF16),
            pltpu.VMEM((G, n, slot, wx + wm), BF16),
            pltpu.VMEM((n, slot, LANES), BF16),
            pltpu.VMEM((n, slot, LANES), BF16),
            pltpu.VMEM((tok, LANES), F32),
            pltpu.VMEM((tok, LANES), F32),
            pltpu.VMEM((wx, tok), F32),
            pltpu.VMEM((blocks, heads, BLOCK), F32),
            pltpu.VMEM((G, wx, tok), BF16),
            pltpu.VMEM((G, rows, wx), F32),
            pltpu.VMEM((blocks - 1, rows, wx), F32),
            pltpu.VMEM((G, rows, wx), F32),
            pltpu.VMEM((G, rows, wx), F32),
            pltpu.VMEM((rows, wx), F32),
            pltpu.VMEM((G, rows, wx), F32),
            pltpu.VMEM((G, states, wx), F32),
            pltpu.VMEM((G, states, wx), F32),
            pltpu.VMEM((states, wx), F32),
            dma((2, G)),
            dma((G,)),
            dma((G,)),
            dma((1,)),
            dma((G, n)),
            dma((G, n)),
            dma((n,)),
            dma((n,)),
            dma((4, G, sub)),
            dma((3, G, sub)),
        ],
        compiler_params=pltpu.CompilerParams(
            collective_id=0, has_side_effects=True, vmem_limit_bytes=VLIM),
        name="prefill",
    )(prompt_sizes, skip_gain, log_rates.reshape(1, head_count), packing,
      inputs, projections, step_sizes)


def solution(mesh):
    in_specs = (
        P(None, ("groups", "ctx")),
        P(None, ("groups", "ctx")),
        P(None, ("groups", "ctx")),
        P(),
        P(),
        P(("groups", "ctx"), None),
        P("groups"),
    )
    out_specs = P(None, ("groups", "ctx"))
    return jax.shard_map(
        functools.partial(per_device, mesh.shape["ctx"]),
        mesh=mesh, in_specs=in_specs, out_specs=out_specs, check_vma=False,
    )
```

```python
import functools
import jax
import jax.numpy as jnp
from jax import lax
from jax.experimental import pallas as pl
from jax.experimental.pallas import tpu as pltpu
from jax.sharding import PartitionSpec as P

G = 4
BLOCK = 128
LANES = 128
PLANE = 4
VLIM = 60 * 1024 * 1024
F32 = jnp.float32
BF16 = jnp.bfloat16
MESH = pl.DeviceIdType.MESH


def dot_nt(a, b):
    return lax.dot_general(a, b, (((1,), (1,)), ((), ())), preferred_element_type=F32)


def starts_of(sizes_ref):
    out = []
    at = jnp.int32(0)
    for s in range(sizes_ref.shape[0]):
        out.append(at)
        at = at + sizes_ref[s]
    return out


def segment_of(position, starts):
    seg = jnp.zeros(position.shape, jnp.int32)
    for at in starts:
        seg = seg + (position >= at).astype(jnp.int32)
    return seg


def decay_of(dt, rate):
    t = dt.shape[0]
    tri = jnp.where(
        lax.broadcasted_iota(jnp.int32, (t, t), 0) >= lax.broadcasted_iota(jnp.int32, (t, t), 1),
        1.0, 0.0).astype(F32)
    return jnp.dot(tri, dt * rate, preferred_element_type=F32, precision=lax.Precision.HIGHEST)


def spread(value, heads, width):
    rows = value.shape[0]
    per = LANES // width
    lane = lax.broadcasted_iota(jnp.int32, (rows, LANES), 1)
    out = []
    for q in range(heads // per):
        acc = jnp.broadcast_to(value[:, q * per:q * per + 1], (rows, LANES))
        for k in range(1, per):
            other = jnp.broadcast_to(value[:, q * per + k:q * per + k + 1], (rows, LANES))
            acc = jnp.where(lane >= k * width, other, acc)
        out.append(acc)
    return jnp.concatenate(out, axis=1)


def group_lanes(value, g, per_group):
    return pltpu.roll(value, lax.rem(LANES - g * per_group, LANES), 1)


def fused_kernel(
    n, heads, width, states, sub,
    sizes_ref, skip_ref, rate_ref, pack_ref, x_hbm, bc_hbm, dt_ref, o_hbm,
    xv, bv, pick, ys, yr, ds, dr, cums, dts, acc, opens, obuf,
    t_ref, t0_ref, early, first, mine, whole, leave, enter, c_ref,
    in_sem, out_sem, own_sem, own_d_sem, xs_sem, xr_sem, dsend_sem, drecv_sem, ssem, rsem,
):
    me = lax.axis_index("ctx")
    tok = dt_ref.shape[1]
    slot = tok // n
    wx = heads * width
    wm = 2 * states
    blocks = tok // BLOCK
    half = n // 2
    q = lax.rem(me, PLANE)
    z = me // PLANE
    nz = n // PLANE
    cw = wx // sub
    starts = starts_of(sizes_ref)
    base = me * tok

    def loop(count, body, low=0):
        def step(i, _):
            body(i)
            return 0
        lax.fori_loop(low, count, step, 0)

    barrier = pltpu.get_barrier_semaphore()
    loop(n, lambda off: pl.semaphore_signal(
        barrier, inc=1, device_id={"ctx": lax.rem(me + off, n)}, device_id_type=MESH), low=1)

    def load(g):
        rx = pl.ds(pl.multiple_of(g * wx, LANES), wx)
        rb = pl.ds(pl.multiple_of(g * wm, LANES), wm)
        return (
            pltpu.make_async_copy(x_hbm.at[rx], xv.at[g], in_sem.at[0, g]),
            pltpu.make_async_copy(bc_hbm.at[rb], bv.at[g], in_sem.at[1, g]),
        )

    def begin(g):
        for part in load(g):
            part.start()

    loop(G, begin)

    rows = lax.broadcasted_iota(jnp.int32, (tok, tok), 0)
    pick[...] = jnp.where(rows == pack_ref[...], 1.0, 0.0).astype(F32).T.astype(BF16)
    head_count = dt_ref.shape[0]
    dt_all = dot_nt(pick[...], dt_ref[...]).astype(BF16)
    dt_all = jnp.concatenate([dt_all, jnp.zeros((tok, LANES - head_count), BF16)], axis=1)
    ds[...] = dt_all.reshape(n, slot, LANES)

    def prep(g):
        for part in load(g):
            part.wait()
        yx = dot_nt(pick[...], xv[g]).astype(BF16)
        yb = dot_nt(pick[...], bv[g]).astype(BF16)
        ys[g, :, :, :wx] = yx.reshape(n, slot, wx)
        ys[g, :, :, wx:] = yb.reshape(n, slot, wm)

    def send_y(g, off):
        to = lax.rem(me + off, n)
        return pltpu.make_async_remote_copy(
            ys.at[g, to], yr.at[g, me], xs_sem.at[g, off], xr_sem.at[g, off],
            device_id={"ctx": to}, device_id_type=MESH)

    def send_d(off):
        to = lax.rem(me + off, n)
        return pltpu.make_async_remote_copy(
            ds.at[to], dr.at[me], dsend_sem.at[off], drecv_sem.at[off],
            device_id={"ctx": to}, device_id_type=MESH)

    def keep_y(g):
        return pltpu.make_async_copy(ys.at[g, me], yr.at[g, me], own_sem.at[g])

    def keep_d():
        return pltpu.make_async_copy(ds.at[me], dr.at[me], own_d_sem.at[0])

    def send_all(g):
        def pair(i):
            send_y(g, half - i).start()

            @pl.when(i > 0)
            def _():
                send_y(g, half + i).start()

        loop(half, pair)
        keep_y(g).start()

    prep(0)
    pl.semaphore_wait(barrier, n - 1)
    loop(n, lambda off: send_d(off).start(), low=1)
    keep_d().start()

    def prep_next(g):
        @pl.when(g < G - 1)
        def _():
            prep(g + 1)
        send_all(g)

    loop(G, prep_next)

    def push(kind, way, g, k, src, dst, to):
        s = pl.ds(pl.multiple_of(k * cw, LANES), cw)
        return pltpu.make_async_remote_copy(
            src.at[g, :, s], dst.at[g, :, s], ssem.at[way, g, k], rsem.at[kind, g, k],
            device_id={"ctx": to}, device_id_type=MESH)

    EARLY, FIRST, ENTER = 0, 1, 2

    def lanes(k):
        return pl.ds(pl.multiple_of(k * cw, LANES), cw)

    def join(old, new):
        gain = new[states:states + 1]
        return jnp.concatenate([gain * old[:states] + new[:states], old[states:] * new[states:]], axis=0)

    def open_stage(g):
        @pl.when((q == 0) | (q == 2))
        def _():
            loop(sub, lambda k: push(EARLY, 0, g, k, t_ref, early, me + 1).start())

    def local_stage(g):
        @pl.when(q == 1)
        def _():
            def up(k):
                s = lanes(k)
                push(EARLY, 0, g, k, t_ref, early, me - 1).wait_recv()
                whole[g, :, s] = join(early[g, :, s], t_ref[g, :, s])
                push(FIRST, 0, g, k, whole, first, me + 2).start()
            loop(sub, up)

        @pl.when(q == 3)
        def _():
            def up(k):
                s = lanes(k)
                push(EARLY, 0, g, k, t_ref, early, me - 1).wait_recv()
                push(FIRST, 0, g, k, first, first, me - 1).wait_recv()
                push(FIRST, 0, g, k, first, first, me - 1).start()
                both = join(first[g, :, s], early[g, :, s])
                mine[g, :, s] = both
                every = join(both, t_ref[g, :, s])
                whole[g, :, s] = every

                @pl.when((z == 0) & (nz > 1))
                def _():
                    leave[g, :, s] = every[:states]
                    push(ENTER, 3, g, k, leave, enter, me + PLANE).start()
            loop(sub, up)

    def carry_stage(g):
        def merge(local, k):
            s = lanes(k)

            @pl.when(z > 0)
            def _():
                c_ref[g, :, s] = local[states:states + 1] * enter[g, :, s] + local[:states]

            @pl.when(z == 0)
            def _():
                c_ref[g, :, s] = local[:states]

        @pl.when(q == 0)
        def _():
            def body(k):
                s = lanes(k)

                @pl.when(z > 0)
                def _():
                    push(ENTER, 1, g, k, enter, enter, me + 1).wait_recv()
                    c_ref[g, :, s] = enter[g, :, s]

                @pl.when(z == 0)
                def _():
                    c_ref[g, :, s] = jnp.zeros((states, cw), F32)
            loop(sub, body)

        @pl.when(q == 1)
        def _():
            def body(k):
                @pl.when(z > 0)
                def _():
                    push(ENTER, 1, g, k, enter, enter, me - 1).wait_recv()
                    push(ENTER, 1, g, k, enter, enter, me - 1).start()
                merge(early[g, :, lanes(k)], k)
            loop(sub, body)

        @pl.when(q == 2)
        def _():
            def body(k):
                push(FIRST, 1, g, k, first, first, me + 1).wait_recv()

                @pl.when(z > 0)
                def _():
                    push(ENTER, 1, g, k, enter, enter, me + 1).wait_recv()
                merge(first[g, :, lanes(k)], k)
            loop(sub, body)

        @pl.when(q == 3)
        def _():
            def body(k):
                s = lanes(k)

                @pl.when(z > 0)
                def _():
                    push(ENTER, 1, g, k, enter, enter, me - 1).wait_recv()

                    @pl.when(z < nz - 1)
                    def _():
                        leave[g, :, s] = (
                            whole[g, states:states + 1, s] * enter[g, :, s] + whole[g, :states, s])
                        push(ENTER, 3, g, k, leave, enter, me + PLANE).start()

                    push(ENTER, 2, g, k, enter, enter, me - 2).start()
                    push(ENTER, 1, g, k, enter, enter, me - 1).start()
                merge(mine[g, :, s], k)
            loop(sub, body)

    def settle(g):
        def one(k):
            @pl.when((q == 0) | (q == 2))
            def _():
                push(EARLY, 0, g, k, t_ref, early, me + 1).wait_send()

            @pl.when(q == 1)
            def _():
                push(FIRST, 0, g, k, whole, first, me + 2).wait_send()

                @pl.when(z > 0)
                def _():
                    push(ENTER, 1, g, k, enter, enter, me - 1).wait_send()

            @pl.when(q == 3)
            def _():
                push(FIRST, 0, g, k, first, first, me - 1).wait_send()

                @pl.when(z < nz - 1)
                def _():
                    push(ENTER, 3, g, k, leave, enter, me + PLANE).wait_send()

                @pl.when(z > 0)
                def _():
                    push(ENTER, 2, g, k, enter, enter, me - 2).wait_send()
                    push(ENTER, 1, g, k, enter, enter, me - 1).wait_send()
        loop(sub, one)

    rate_all = jnp.concatenate(
        [rate_ref[...], jnp.zeros((1, LANES - head_count), F32)], axis=1)
    rate_all = jnp.broadcast_to(-jnp.exp(rate_all), (8, LANES))

    def rows_of(b):
        return slice(b * BLOCK // slot, (b + 1) * BLOCK // slot)

    def y_of(g, b, lo, hi):
        return yr[g, rows_of(b), :, lo:hi].reshape(BLOCK, hi - lo)

    def states_stage(g):
        rate = group_lanes(rate_all, g, heads)[0:1]
        total = None
        for b in range(blocks):
            lo = b * BLOCK
            head = base + lo
            last = head + BLOCK - 1
            dt = dr[rows_of(b)].reshape(BLOCK, LANES).astype(F32)
            dt = group_lanes(dt, g, heads)
            cum = decay_of(dt, rate)
            cums[lo:lo + BLOCK, :] = cum
            dts[lo:lo + BLOCK, :] = dt
            end = cum[BLOCK - 1:BLOCK, :]
            pos = head + lax.broadcasted_iota(jnp.int32, (BLOCK, LANES), 0)
            last_seg = jnp.int32(0)
            cut = jnp.int32(0)
            for at in starts:
                last_seg = last_seg + (last >= at).astype(jnp.int32)
                cut = cut + ((at >= head) & (at <= last)).astype(jnp.int32)
            same = segment_of(pos, starts) == last_seg
            into = jnp.where(same, jnp.exp(end - cum), 0.0) * dt
            weighted = (y_of(g, b, 0, wx).astype(F32) * spread(into, heads, width)).astype(BF16)
            maps_t = y_of(g, b, wx, wx + wm).astype(F32).T
            in_map = maps_t[:states].astype(BF16)
            block_total = jnp.dot(in_map, weighted, preferred_element_type=F32)
            keep_h = jnp.where(cut == 0, jnp.exp(end), 0.0)
            keep = spread(jnp.broadcast_to(keep_h, (8, LANES)), heads, width)
            if total is None:
                total, gain = block_total, keep
            else:
                total = keep[0:1] * total + block_total
                gain = gain * keep
            if b < blocks - 1:
                t0_ref[g, b, :states, :] = block_total
                t0_ref[g, b, states:, :] = keep
        t_ref[g, :states, :] = total
        t_ref[g, states:, :] = gain

    def inner_stage(g):
        for b in range(blocks):
            lo = b * BLOCK
            head = base + lo
            cum = cums[lo:lo + BLOCK, :]
            cum_t = cum.T
            dt_t = dts[lo:lo + BLOCK, :].T
            pos_i = head + lax.broadcasted_iota(jnp.int32, (BLOCK, BLOCK), 0)
            pos_j = head + lax.broadcasted_iota(jnp.int32, (BLOCK, BLOCK), 1)
            allowed = (pos_i >= pos_j) & (segment_of(pos_i, starts) == segment_of(pos_j, starts))
            row_pos = head + lax.broadcasted_iota(jnp.int32, (1, BLOCK), 1)
            cut = jnp.zeros((1, BLOCK), jnp.int32)
            for at in starts:
                cut = cut + ((row_pos >= at) & (at >= head)).astype(jnp.int32)
            opens[g, b] = jnp.where(cut == 0, jnp.exp(cum_t[:heads]), 0.0)
            in_map = y_of(g, b, wx, wx + states)
            out_map = y_of(g, b, wx + states, wx + wm)
            gram = dot_nt(out_map, in_map)
            x_fm = y_of(g, b, 0, wx).T
            for h in range(heads):
                gap = jnp.broadcast_to(cum[:, h:h + 1], (BLOCK, BLOCK)) - cum_t[h:h + 1]
                mask = jnp.exp(jnp.where(allowed, gap, -jnp.inf))
                mixing = (gram * (mask * dt_t[h:h + 1])).astype(BF16)
                r = slice(h * width, (h + 1) * width)
                xh = x_fm[r]
                acc[g, r, lo:lo + BLOCK] = (
                    dot_nt(xh, mixing) + skip_ref[g * heads + h] * xh.astype(F32))

    def store_out(g):
        return pltpu.make_async_copy(
            obuf.at[g], o_hbm.at[pl.ds(pl.multiple_of(g * wx, LANES), wx)], out_sem.at[g])

    def output_stage(g):
        carry = c_ref[g]
        for b in range(blocks):
            lo = b * BLOCK
            out_map = y_of(g, b, wx + states, wx + wm)
            carried = dot_nt(carry.astype(BF16).T, out_map)
            for h in range(heads):
                r = slice(h * width, (h + 1) * width)
                obuf[g, r, lo:lo + BLOCK] = (
                    acc[g, r, lo:lo + BLOCK] + carried[r] * opens[g, b, h:h + 1]).astype(BF16)
            if b < blocks - 1:
                carry = t0_ref[g, b, states:states + 1, :] * carry + t0_ref[g, b, :states, :]
        store_out(g).start()

    loop(n, lambda off: send_d(off).wait_recv(), low=1)
    keep_d().wait()

    ahead = z < nz // 2

    def turn(g):
        @pl.when(ahead & (g == G - 1))
        def _():
            loop(G - 1, carry_stage)

        loop(n, lambda off: send_y(g, off).wait_recv(), low=1)
        keep_y(g).wait()
        states_stage(g)
        open_stage(g)

        @pl.when(g == G - 1)
        def _():
            local_stage(g)

        inner_stage(g)

        @pl.when(g < G - 1)
        def _():
            local_stage(g)

    loop(G, turn)

    @pl.when(ahead)
    def _():
        carry_stage(G - 1)

    def wrap(g):
        @pl.when(jnp.logical_not(ahead))
        def _():
            carry_stage(g)
        output_stage(g)

    loop(G, wrap)
    loop(n, lambda off: send_d(off).wait_send(), low=1)

    def close(g):
        loop(n, lambda off: send_y(g, off).wait_send(), low=1)
        settle(g)
        store_out(g).wait()

    loop(G, close)


def per_device(n, inputs, projections, step_sizes, log_rates, skip_gain, packing, prompt_sizes):
    tok = inputs.shape[1]
    head_count = log_rates.shape[0]
    heads = head_count // G
    states = projections.shape[0] // (2 * G)
    width = inputs.shape[0] // head_count
    wx = heads * width
    wm = 2 * states
    slot = tok // n
    blocks = tok // BLOCK
    rows = states + 8
    sub = 4
    vmem = pl.BlockSpec(memory_space=pltpu.VMEM)
    smem = pl.BlockSpec(memory_space=pltpu.SMEM)
    hbm = pl.BlockSpec(memory_space=pl.ANY)
    dma = pltpu.SemaphoreType.DMA
    return pl.pallas_call(
        functools.partial(fused_kernel, n, heads, width, states, sub),
        in_specs=[smem, smem, vmem, vmem, hbm, hbm, vmem],
        out_specs=hbm,
        out_shape=jax.ShapeDtypeStruct((G * wx, tok), BF16),
        scratch_shapes=[
            pltpu.VMEM((G, wx, tok), BF16),
            pltpu.VMEM((G, wm, tok), BF16),
            pltpu.VMEM((tok, tok), BF16),
            pltpu.VMEM((G, n, slot, wx + wm), BF16),
            pltpu.VMEM((G, n, slot, wx + wm), BF16),
            pltpu.VMEM((n, slot, LANES), BF16),
            pltpu.VMEM((n, slot, LANES), BF16),
            pltpu.VMEM((tok, LANES), F32),
            pltpu.VMEM((tok, LANES), F32),
            pltpu.VMEM((G, wx, tok), F32),
            pltpu.VMEM((G, blocks, heads, BLOCK), F32),
            pltpu.VMEM((G, wx, tok), BF16),
            pltpu.VMEM((G, rows, wx), F32),
            pltpu.VMEM((G, blocks - 1, rows, wx), F32),
            pltpu.VMEM((G, rows, wx), F32),
            pltpu.VMEM((G, rows, wx), F32),
            pltpu.VMEM((G, rows, wx), F32),
            pltpu.VMEM((G, rows, wx), F32),
            pltpu.VMEM((G, states, wx), F32),
            pltpu.VMEM((G, states, wx), F32),
            pltpu.VMEM((G, states, wx), F32),
            dma((2, G)),
            dma((G,)),
            dma((G,)),
            dma((1,)),
            dma((G, n)),
            dma((G, n)),
            dma((n,)),
            dma((n,)),
            dma((4, G, sub)),
            dma((3, G, sub)),
        ],
        compiler_params=pltpu.CompilerParams(
            collective_id=0, has_side_effects=True, vmem_limit_bytes=VLIM),
        name="prefill",
    )(prompt_sizes, skip_gain, log_rates.reshape(1, head_count), packing,
      inputs, projections, step_sizes)


def solution(mesh):
    in_specs = (
        P(None, ("groups", "ctx")),
        P(None, ("groups", "ctx")),
        P(None, ("groups", "ctx")),
        P(),
        P(),
        P(("groups", "ctx"), None),
        P("groups"),
    )
    out_specs = P(None, ("groups", "ctx"))
    return jax.shard_map(
        functools.partial(per_device, mesh.shape["ctx"]),
        mesh=mesh, in_specs=in_specs, out_specs=out_specs, check_vma=False,
    )
```

```python
import functools
import jax
import jax.numpy as jnp
from jax import lax
from jax.experimental import pallas as pl
from jax.experimental.pallas import tpu as pltpu
from jax.sharding import PartitionSpec as P

G = 4
BLOCK = 128
LANES = 128
PLANE = 4
VLIM = 36 * 1024 * 1024
F32 = jnp.float32
BF16 = jnp.bfloat16
MESH = pl.DeviceIdType.MESH


def dot_nt(a, b):
    return lax.dot_general(a, b, (((1,), (1,)), ((), ())), preferred_element_type=F32)


def starts_of(sizes_ref):
    out = []
    at = jnp.int32(0)
    for s in range(sizes_ref.shape[0]):
        out.append(at)
        at = at + sizes_ref[s]
    return out


def segment_of(position, starts):
    seg = jnp.zeros(position.shape, jnp.int32)
    for at in starts:
        seg = seg + (position >= at).astype(jnp.int32)
    return seg


def decay_of(dt, rate):
    t = dt.shape[0]
    tri = jnp.where(
        lax.broadcasted_iota(jnp.int32, (t, t), 0) >= lax.broadcasted_iota(jnp.int32, (t, t), 1),
        1.0, 0.0).astype(F32)
    return jnp.dot(tri, dt * rate, preferred_element_type=F32, precision=lax.Precision.HIGHEST)


def spread(value, heads, width):
    rows = value.shape[0]
    per = LANES // width
    lane = lax.broadcasted_iota(jnp.int32, (rows, LANES), 1)
    out = []
    for q in range(heads // per):
        acc = jnp.broadcast_to(value[:, q * per:q * per + 1], (rows, LANES))
        for k in range(1, per):
            other = jnp.broadcast_to(value[:, q * per + k:q * per + k + 1], (rows, LANES))
            acc = jnp.where(lane >= k * width, other, acc)
        out.append(acc)
    return jnp.concatenate(out, axis=1)


def group_lanes(value, g, per_group):
    return pltpu.roll(value, lax.rem(LANES - g * per_group, LANES), 1)


def fused_kernel(
    n, heads, width, states, sub,
    sizes_hbm, skip_hbm, rate_hbm, pack_hbm, x_hbm, bc_hbm, dt_hbm, o_hbm,
    sizes_ref, skip_ref, rate_ref, pack_ref, dt_ref,
    xv, bv, pick, ys, yr, ds, dr, cums, dts, acc, opens, obuf,
    t_ref, t0_ref, early, first, mine, whole, leave, enter, c_ref,
    in_sem, few_sem, out_sem, own_sem, own_d_sem, xs_sem, xr_sem, dsend_sem, drecv_sem, ssem, rsem,
):
    me = lax.axis_index("ctx")
    tok = dt_ref.shape[1]
    slot = tok // n
    wx = heads * width
    wm = 2 * states
    blocks = tok // BLOCK
    half = n // 2
    q = lax.rem(me, PLANE)
    z = me // PLANE
    nz = n // PLANE
    cw = wx // sub
    base = me * tok

    def loop(count, body, low=0):
        def step(i, _):
            body(i)
            return 0
        lax.fori_loop(low, count, step, 0)

    barrier = pltpu.get_barrier_semaphore()
    loop(n, lambda off: pl.semaphore_signal(
        barrier, inc=1, device_id={"ctx": lax.rem(me + off, n)}, device_id_type=MESH), low=1)

    def load(g):
        rx = pl.ds(pl.multiple_of(g * wx, LANES), wx)
        rb = pl.ds(pl.multiple_of(g * wm, LANES), wm)
        return (
            pltpu.make_async_copy(x_hbm.at[rx], xv.at[g], in_sem.at[0, g]),
            pltpu.make_async_copy(bc_hbm.at[rb], bv.at[g], in_sem.at[1, g]),
        )

    def begin(g):
        for part in load(g):
            part.start()

    few = [
        pltpu.make_async_copy(src, dst, few_sem.at[i])
        for i, (src, dst) in enumerate((
            (pack_hbm, pack_ref), (dt_hbm, dt_ref), (sizes_hbm, sizes_ref),
            (skip_hbm, skip_ref), (rate_hbm, rate_ref)))
    ]
    few[0].start()
    few[1].start()
    loop(G, begin)
    for part in few[2:]:
        part.start()
    few[0].wait()

    rows = lax.broadcasted_iota(jnp.int32, (tok, tok), 0)
    pick[...] = jnp.where(rows == pack_ref[...], 1.0, 0.0).astype(F32).T.astype(BF16)
    head_count = dt_ref.shape[0]
    few[1].wait()
    dt_all = dot_nt(pick[...], dt_ref[...]).astype(BF16)
    dt_all = jnp.concatenate([dt_all, jnp.zeros((tok, LANES - head_count), BF16)], axis=1)
    ds[...] = dt_all.reshape(n, slot, LANES)

    def prep(g):
        for part in load(g):
            part.wait()
        yx = dot_nt(pick[...], xv[g]).astype(BF16)
        yb = dot_nt(pick[...], bv[g]).astype(BF16)
        ys[g, :, :, :wx] = yx.reshape(n, slot, wx)
        ys[g, :, :, wx:] = yb.reshape(n, slot, wm)

    def send_y(g, off):
        to = lax.rem(me + off, n)
        return pltpu.make_async_remote_copy(
            ys.at[g, to], yr.at[g, me], xs_sem.at[g, off], xr_sem.at[g, off],
            device_id={"ctx": to}, device_id_type=MESH)

    def send_d(off):
        to = lax.rem(me + off, n)
        return pltpu.make_async_remote_copy(
            ds.at[to], dr.at[me], dsend_sem.at[off], drecv_sem.at[off],
            device_id={"ctx": to}, device_id_type=MESH)

    def keep_y(g):
        return pltpu.make_async_copy(ys.at[g, me], yr.at[g, me], own_sem.at[g])

    def keep_d():
        return pltpu.make_async_copy(ds.at[me], dr.at[me], own_d_sem.at[0])

    def send_all(g):
        def pair(i):
            send_y(g, half - i).start()

            @pl.when(i > 0)
            def _():
                send_y(g, half + i).start()

        loop(half, pair)
        keep_y(g).start()

    prep(0)
    pl.semaphore_wait(barrier, n - 1)
    loop(n, lambda off: send_d(off).start(), low=1)
    keep_d().start()

    def prep_next(g):
        @pl.when(g < G - 1)
        def _():
            prep(g + 1)
        send_all(g)

    loop(G, prep_next)

    def push(kind, way, g, k, src, dst, to):
        s = pl.ds(pl.multiple_of(k * cw, LANES), cw)
        return pltpu.make_async_remote_copy(
            src.at[g, :, s], dst.at[g, :, s], ssem.at[way, g, k], rsem.at[kind, g, k],
            device_id={"ctx": to}, device_id_type=MESH)

    EARLY, FIRST, ENTER = 0, 1, 2

    def lanes(k):
        return pl.ds(pl.multiple_of(k * cw, LANES), cw)

    def join(old, new):
        gain = new[states:states + 1]
        return jnp.concatenate([gain * old[:states] + new[:states], old[states:] * new[states:]], axis=0)

    def open_stage(g):
        @pl.when((q == 0) | (q == 2))
        def _():
            loop(sub, lambda k: push(EARLY, 0, g, k, t_ref, early, me + 1).start())

    def local_stage(g):
        @pl.when(q == 1)
        def _():
            def up(k):
                s = lanes(k)
                push(EARLY, 0, g, k, t_ref, early, me - 1).wait_recv()
                whole[g, :, s] = join(early[g, :, s], t_ref[g, :, s])
                push(FIRST, 0, g, k, whole, first, me + 2).start()
            loop(sub, up)

        @pl.when(q == 3)
        def _():
            def up(k):
                s = lanes(k)
                push(EARLY, 0, g, k, t_ref, early, me - 1).wait_recv()
                push(FIRST, 0, g, k, first, first, me - 1).wait_recv()
                push(FIRST, 0, g, k, first, first, me - 1).start()
                both = join(first[g, :, s], early[g, :, s])
                mine[g, :, s] = both
                every = join(both, t_ref[g, :, s])
                whole[g, :, s] = every

                @pl.when((z == 0) & (nz > 1))
                def _():
                    leave[g, :, s] = every[:states]
                    push(ENTER, 3, g, k, leave, enter, me + PLANE).start()
            loop(sub, up)

    def carry_stage(g):
        def merge(local, k):
            s = lanes(k)

            @pl.when(z > 0)
            def _():
                c_ref[g, :, s] = local[states:states + 1] * enter[g, :, s] + local[:states]

            @pl.when(z == 0)
            def _():
                c_ref[g, :, s] = local[:states]

        @pl.when(q == 0)
        def _():
            def body(k):
                s = lanes(k)

                @pl.when(z > 0)
                def _():
                    push(ENTER, 1, g, k, enter, enter, me + 1).wait_recv()
                    c_ref[g, :, s] = enter[g, :, s]

                @pl.when(z == 0)
                def _():
                    c_ref[g, :, s] = jnp.zeros((states, cw), F32)
            loop(sub, body)

        @pl.when(q == 1)
        def _():
            def body(k):
                @pl.when(z > 0)
                def _():
                    push(ENTER, 1, g, k, enter, enter, me - 1).wait_recv()
                    push(ENTER, 1, g, k, enter, enter, me - 1).start()
                merge(early[g, :, lanes(k)], k)
            loop(sub, body)

        @pl.when(q == 2)
        def _():
            def body(k):
                push(FIRST, 1, g, k, first, first, me + 1).wait_recv()

                @pl.when(z > 0)
                def _():
                    push(ENTER, 1, g, k, enter, enter, me + 1).wait_recv()
                merge(first[g, :, lanes(k)], k)
            loop(sub, body)

        @pl.when(q == 3)
        def _():
            def body(k):
                s = lanes(k)

                @pl.when(z > 0)
                def _():
                    push(ENTER, 1, g, k, enter, enter, me - 1).wait_recv()

                    @pl.when(z < nz - 1)
                    def _():
                        leave[g, :, s] = (
                            whole[g, states:states + 1, s] * enter[g, :, s] + whole[g, :states, s])
                        push(ENTER, 3, g, k, leave, enter, me + PLANE).start()

                    push(ENTER, 2, g, k, enter, enter, me - 2).start()
                    push(ENTER, 1, g, k, enter, enter, me - 1).start()
                merge(mine[g, :, s], k)
            loop(sub, body)

    def settle(g):
        def one(k):
            @pl.when((q == 0) | (q == 2))
            def _():
                push(EARLY, 0, g, k, t_ref, early, me + 1).wait_send()

            @pl.when(q == 1)
            def _():
                push(FIRST, 0, g, k, whole, first, me + 2).wait_send()

                @pl.when(z > 0)
                def _():
                    push(ENTER, 1, g, k, enter, enter, me - 1).wait_send()

            @pl.when(q == 3)
            def _():
                push(FIRST, 0, g, k, first, first, me - 1).wait_send()

                @pl.when(z < nz - 1)
                def _():
                    push(ENTER, 3, g, k, leave, enter, me + PLANE).wait_send()

                @pl.when(z > 0)
                def _():
                    push(ENTER, 2, g, k, enter, enter, me - 2).wait_send()
                    push(ENTER, 1, g, k, enter, enter, me - 1).wait_send()
        loop(sub, one)

    for part in few[2:]:
        part.wait()
    starts = starts_of(sizes_ref)
    rate_all = jnp.concatenate(
        [rate_ref[...], jnp.zeros((1, LANES - head_count), F32)], axis=1)
    rate_all = jnp.broadcast_to(-jnp.exp(rate_all), (8, LANES))

    def rows_of(b):
        return slice(b * BLOCK // slot, (b + 1) * BLOCK // slot)

    def y_of(g, b, lo, hi):
        return yr[g, rows_of(b), :, lo:hi].reshape(BLOCK, hi - lo)

    def states_stage(g):
        rate = group_lanes(rate_all, g, heads)[0:1]
        total = None
        for b in range(blocks):
            lo = b * BLOCK
            head = base + lo
            last = head + BLOCK - 1
            dt = dr[rows_of(b)].reshape(BLOCK, LANES).astype(F32)
            dt = group_lanes(dt, g, heads)
            cum = decay_of(dt, rate)
            cums[lo:lo + BLOCK, :] = cum
            dts[lo:lo + BLOCK, :] = dt
            end = cum[BLOCK - 1:BLOCK, :]
            pos = head + lax.broadcasted_iota(jnp.int32, (BLOCK, LANES), 0)
            last_seg = jnp.int32(0)
            cut = jnp.int32(0)
            for at in starts:
                last_seg = last_seg + (last >= at).astype(jnp.int32)
                cut = cut + ((at >= head) & (at <= last)).astype(jnp.int32)
            same = segment_of(pos, starts) == last_seg
            into = jnp.where(same, jnp.exp(end - cum), 0.0) * dt
            weighted = (y_of(g, b, 0, wx).astype(F32) * spread(into, heads, width)).astype(BF16)
            maps_t = y_of(g, b, wx, wx + wm).astype(F32).T
            in_map = maps_t[:states].astype(BF16)
            block_total = jnp.dot(in_map, weighted, preferred_element_type=F32)
            keep_h = jnp.where(cut == 0, jnp.exp(end), 0.0)
            keep = spread(jnp.broadcast_to(keep_h, (8, LANES)), heads, width)
            if total is None:
                total, gain = block_total, keep
            else:
                total = keep[0:1] * total + block_total
                gain = gain * keep
            if b < blocks - 1:
                t0_ref[g, b, :states, :] = block_total
                t0_ref[g, b, states:, :] = keep
        t_ref[g, :states, :] = total
        t_ref[g, states:, :] = gain

    def inner_stage(g):
        for b in range(blocks):
            lo = b * BLOCK
            head = base + lo
            cum = cums[lo:lo + BLOCK, :]
            cum_t = cum.T
            dt_t = dts[lo:lo + BLOCK, :].T
            pos_i = head + lax.broadcasted_iota(jnp.int32, (BLOCK, BLOCK), 0)
            pos_j = head + lax.broadcasted_iota(jnp.int32, (BLOCK, BLOCK), 1)
            allowed = (pos_i >= pos_j) & (segment_of(pos_i, starts) == segment_of(pos_j, starts))
            row_pos = head + lax.broadcasted_iota(jnp.int32, (1, BLOCK), 1)
            cut = jnp.zeros((1, BLOCK), jnp.int32)
            for at in starts:
                cut = cut + ((row_pos >= at) & (at >= head)).astype(jnp.int32)
            opens[g, b] = jnp.where(cut == 0, jnp.exp(cum_t[:heads]), 0.0)
            in_map = y_of(g, b, wx, wx + states)
            out_map = y_of(g, b, wx + states, wx + wm)
            gram = dot_nt(out_map, in_map)
            x_fm = y_of(g, b, 0, wx).T
            for h in range(heads):
                gap = jnp.broadcast_to(cum[:, h:h + 1], (BLOCK, BLOCK)) - cum_t[h:h + 1]
                mask = jnp.exp(jnp.where(allowed, gap, -jnp.inf))
                mixing = (gram * (mask * dt_t[h:h + 1])).astype(BF16)
                r = slice(h * width, (h + 1) * width)
                xh = x_fm[r]
                acc[g, r, lo:lo + BLOCK] = (
                    dot_nt(xh, mixing) + skip_ref[g * heads + h] * xh.astype(F32))

    def store_out(g):
        return pltpu.make_async_copy(
            obuf.at[g], o_hbm.at[pl.ds(pl.multiple_of(g * wx, LANES), wx)], out_sem.at[g])

    def output_stage(g):
        carry = c_ref[g]
        for b in range(blocks):
            lo = b * BLOCK
            out_map = y_of(g, b, wx + states, wx + wm)
            carried = dot_nt(carry.astype(BF16).T, out_map)
            for h in range(heads):
                r = slice(h * width, (h + 1) * width)
                obuf[g, r, lo:lo + BLOCK] = (
                    acc[g, r, lo:lo + BLOCK] + carried[r] * opens[g, b, h:h + 1]).astype(BF16)
            if b < blocks - 1:
                carry = t0_ref[g, b, states:states + 1, :] * carry + t0_ref[g, b, :states, :]
        store_out(g).start()

    loop(n, lambda off: send_d(off).wait_recv(), low=1)
    keep_d().wait()

    final = z == nz - 1
    ahead = (z < nz // 2) & jnp.logical_not(final)

    def turn(g):
        @pl.when(ahead & (g == G - 1))
        def _():
            loop(G - 1, carry_stage)

        loop(n, lambda off: send_y(g, off).wait_recv(), low=1)
        keep_y(g).wait()
        states_stage(g)
        open_stage(g)

        @pl.when(g == G - 1)
        def _():
            local_stage(g)

            @pl.when(jnp.logical_not(final))
            def _():
                loop(G, carry_stage, low=jnp.where(ahead, G - 1, 0))

        inner_stage(g)

        @pl.when(g < G - 1)
        def _():
            local_stage(g)

    loop(G, turn)

    def wrap(g):
        @pl.when(final)
        def _():
            carry_stage(g)
        output_stage(g)

    loop(G, wrap)
    loop(n, lambda off: send_d(off).wait_send(), low=1)

    def close(g):
        loop(n, lambda off: send_y(g, off).wait_send(), low=1)
        settle(g)
        store_out(g).wait()

    loop(G, close)


def per_device(n, inputs, projections, step_sizes, log_rates, skip_gain, packing, prompt_sizes):
    tok = inputs.shape[1]
    head_count = log_rates.shape[0]
    heads = head_count // G
    states = projections.shape[0] // (2 * G)
    width = inputs.shape[0] // head_count
    wx = heads * width
    wm = 2 * states
    slot = tok // n
    blocks = tok // BLOCK
    rows = states + 8
    sub = 4
    hbm = pl.BlockSpec(memory_space=pltpu.HBM)
    dma = pltpu.SemaphoreType.DMA
    return pl.pallas_call(
        functools.partial(fused_kernel, n, heads, width, states, sub),
        in_specs=[hbm] * 7,
        out_specs=pl.BlockSpec(memory_space=pl.ANY),
        out_shape=jax.ShapeDtypeStruct((G * wx, tok), BF16),
        scratch_shapes=[
            pltpu.SMEM(prompt_sizes.shape, jnp.int32),
            pltpu.SMEM(skip_gain.shape, F32),
            pltpu.VMEM((1, head_count), F32),
            pltpu.VMEM((1, tok), jnp.int32),
            pltpu.VMEM((head_count, tok), BF16),
            pltpu.VMEM((G, wx, tok), BF16),
            pltpu.VMEM((G, wm, tok), BF16),
            pltpu.VMEM((tok, tok), BF16),
            pltpu.VMEM((G, n, slot, wx + wm), BF16),
            pltpu.VMEM((G, n, slot, wx + wm), BF16),
            pltpu.VMEM((n, slot, LANES), BF16),
            pltpu.VMEM((n, slot, LANES), BF16),
            pltpu.VMEM((tok, LANES), F32),
            pltpu.VMEM((tok, LANES), F32),
            pltpu.VMEM((G, wx, tok), F32),
            pltpu.VMEM((G, blocks, heads, BLOCK), F32),
            pltpu.VMEM((G, wx, tok), BF16),
            pltpu.VMEM((G, rows, wx), F32),
            pltpu.VMEM((G, blocks - 1, rows, wx), F32),
            pltpu.VMEM((G, rows, wx), F32),
            pltpu.VMEM((G, rows, wx), F32),
            pltpu.VMEM((G, rows, wx), F32),
            pltpu.VMEM((G, rows, wx), F32),
            pltpu.VMEM((G, states, wx), F32),
            pltpu.VMEM((G, states, wx), F32),
            pltpu.VMEM((G, states, wx), F32),
            dma((2, G)),
            dma((5,)),
            dma((G,)),
            dma((G,)),
            dma((1,)),
            dma((G, n)),
            dma((G, n)),
            dma((n,)),
            dma((n,)),
            dma((4, G, sub)),
            dma((3, G, sub)),
        ],
        compiler_params=pltpu.CompilerParams(
            collective_id=0, has_side_effects=True, vmem_limit_bytes=VLIM),
        name="prefill",
    )(*[pltpu.with_memory_space_constraint(part, pltpu.HBM) for part in (
        prompt_sizes, skip_gain, log_rates.reshape(1, head_count), packing,
        inputs, projections, step_sizes)])


def solution(mesh):
    in_specs = (
        P(None, ("groups", "ctx")),
        P(None, ("groups", "ctx")),
        P(None, ("groups", "ctx")),
        P(),
        P(),
        P(("groups", "ctx"), None),
        P("groups"),
    )
    out_specs = P(None, ("groups", "ctx"))
    return jax.shard_map(
        functools.partial(per_device, mesh.shape["ctx"]),
        mesh=mesh, in_specs=in_specs, out_specs=out_specs, check_vma=False,
    )
```

```python
import functools
import jax
import jax.numpy as jnp
from jax import lax
from jax.experimental import pallas as pl
from jax.experimental.pallas import tpu as pltpu
from jax.sharding import PartitionSpec as P

G = 4
BLOCK = 128
LANES = 128
PLANE = 4
VLIM = 36 * 1024 * 1024
F32 = jnp.float32
BF16 = jnp.bfloat16
MESH = pl.DeviceIdType.MESH


def dot_nt(a, b):
    return lax.dot_general(a, b, (((1,), (1,)), ((), ())), preferred_element_type=F32)


def starts_of(sizes_ref):
    out = []
    at = jnp.int32(0)
    for s in range(sizes_ref.shape[0]):
        out.append(at)
        at = at + sizes_ref[s]
    return out


def segment_of(position, starts):
    seg = jnp.zeros(position.shape, jnp.int32)
    for at in starts:
        seg = seg + (position >= at).astype(jnp.int32)
    return seg


def decay_of(dt, rate):
    t = dt.shape[0]
    tri = jnp.where(
        lax.broadcasted_iota(jnp.int32, (t, t), 0) >= lax.broadcasted_iota(jnp.int32, (t, t), 1),
        1.0, 0.0).astype(F32)
    return jnp.dot(tri, dt * rate, preferred_element_type=F32, precision=lax.Precision.HIGHEST)


def spread(value, heads, width):
    rows = value.shape[0]
    per = LANES // width
    lane = lax.broadcasted_iota(jnp.int32, (rows, LANES), 1)
    out = []
    for q in range(heads // per):
        acc = jnp.broadcast_to(value[:, q * per:q * per + 1], (rows, LANES))
        for k in range(1, per):
            other = jnp.broadcast_to(value[:, q * per + k:q * per + k + 1], (rows, LANES))
            acc = jnp.where(lane >= k * width, other, acc)
        out.append(acc)
    return jnp.concatenate(out, axis=1)


def group_lanes(value, g, per_group):
    return pltpu.roll(value, lax.rem(LANES - g * per_group, LANES), 1)


def fused_kernel(
    n, heads, width, states, sub,
    sizes_hbm, skip_hbm, rate_hbm, pack_hbm, x_hbm, bc_hbm, dt_hbm, o_hbm,
    sizes_ref, skip_ref, rate_ref, pack_ref, dt_ref,
    xv, bv, pick, ys, yr, ds, dr, cums, dts, acc, opens, obuf,
    t_ref, t0_ref, early, first, mine, whole, leave, enter, c_ref,
    in_sem, few_sem, out_sem, own_sem, own_d_sem, xs_sem, xr_sem, dsend_sem, drecv_sem, ssem, rsem,
):
    me = lax.axis_index("ctx")
    tok = dt_ref.shape[1]
    slot = tok // n
    wx = heads * width
    wm = 2 * states
    blocks = tok // BLOCK
    half = n // 2
    q = lax.rem(me, PLANE)
    z = me // PLANE
    nz = n // PLANE
    cw = wx // sub
    base = me * tok

    def loop(count, body, low=0):
        def step(i, _):
            body(i)
            return 0
        lax.fori_loop(low, count, step, 0)

    barrier = pltpu.get_barrier_semaphore()
    loop(n, lambda off: pl.semaphore_signal(
        barrier, inc=1, device_id={"ctx": lax.rem(me + off, n)}, device_id_type=MESH), low=1)

    def load(g):
        rx = pl.ds(pl.multiple_of(g * wx, LANES), wx)
        rb = pl.ds(pl.multiple_of(g * wm, LANES), wm)
        return (
            pltpu.make_async_copy(x_hbm.at[rx], xv.at[g], in_sem.at[0, g]),
            pltpu.make_async_copy(bc_hbm.at[rb], bv.at[g], in_sem.at[1, g]),
        )

    def begin(g):
        for part in load(g):
            part.start()

    few = [
        pltpu.make_async_copy(src, dst, few_sem.at[i])
        for i, (src, dst) in enumerate((
            (pack_hbm, pack_ref), (dt_hbm, dt_ref), (sizes_hbm, sizes_ref),
            (skip_hbm, skip_ref), (rate_hbm, rate_ref)))
    ]
    few[0].start()
    few[1].start()
    loop(G, begin)
    for part in few[2:]:
        part.start()
    few[0].wait()

    rows = lax.broadcasted_iota(jnp.int32, (tok, tok), 0)
    pick[...] = jnp.where(rows == pack_ref[...], 1.0, 0.0).astype(F32).T.astype(BF16)
    head_count = dt_ref.shape[0]
    few[1].wait()
    dt_all = dot_nt(pick[...], dt_ref[...]).astype(BF16)
    dt_all = jnp.concatenate([dt_all, jnp.zeros((tok, LANES - head_count), BF16)], axis=1)
    ds[...] = dt_all.reshape(n, slot, LANES)

    def prep(g):
        for part in load(g):
            part.wait()
        yx = dot_nt(pick[...], xv[g]).astype(BF16)
        yb = dot_nt(pick[...], bv[g]).astype(BF16)
        ys[g, :, :, :wx] = yx.reshape(n, slot, wx)
        ys[g, :, :, wx:] = yb.reshape(n, slot, wm)

    def send_y(g, off):
        to = lax.rem(me + off, n)
        return pltpu.make_async_remote_copy(
            ys.at[g, to], yr.at[g, me], xs_sem.at[g, off], xr_sem.at[g, off],
            device_id={"ctx": to}, device_id_type=MESH)

    def send_d(off):
        to = lax.rem(me + off, n)
        return pltpu.make_async_remote_copy(
            ds.at[to], dr.at[me], dsend_sem.at[off], drecv_sem.at[off],
            device_id={"ctx": to}, device_id_type=MESH)

    def keep_y(g):
        return pltpu.make_async_copy(ys.at[g, me], yr.at[g, me], own_sem.at[g])

    def keep_d():
        return pltpu.make_async_copy(ds.at[me], dr.at[me], own_d_sem.at[0])

    def send_all(g):
        def pair(i):
            send_y(g, half - i).start()

            @pl.when(i > 0)
            def _():
                send_y(g, half + i).start()

        loop(half, pair)
        keep_y(g).start()

    prep(0)
    pl.semaphore_wait(barrier, n - 1)
    loop(n, lambda off: send_d(off).start(), low=1)
    keep_d().start()

    def prep_next(g):
        @pl.when(g < G - 1)
        def _():
            prep(g + 1)
        send_all(g)

    loop(G, prep_next)

    def push(kind, way, g, k, src, dst, to):
        s = pl.ds(pl.multiple_of(k * cw, LANES), cw)
        return pltpu.make_async_remote_copy(
            src.at[g, :, s], dst.at[g, :, s], ssem.at[way, g, k], rsem.at[kind, g, k],
            device_id={"ctx": to}, device_id_type=MESH)

    EARLY, FIRST, ENTER = 0, 1, 2

    def lanes(k):
        return pl.ds(pl.multiple_of(k * cw, LANES), cw)

    def join(old, new):
        gain = new[states:states + 1]
        return jnp.concatenate([gain * old[:states] + new[:states], old[states:] * new[states:]], axis=0)

    def open_stage(g):
        @pl.when((q == 0) | (q == 2))
        def _():
            loop(sub, lambda k: push(EARLY, 0, g, k, t_ref, early, me + 1).start())

    def local_stage(g):
        @pl.when(q == 1)
        def _():
            def up(k):
                s = lanes(k)
                push(EARLY, 0, g, k, t_ref, early, me - 1).wait_recv()
                whole[g, :, s] = join(early[g, :, s], t_ref[g, :, s])
                push(FIRST, 0, g, k, whole, first, me + 2).start()
            loop(sub, up)

        @pl.when(q == 3)
        def _():
            def up(k):
                s = lanes(k)
                push(EARLY, 0, g, k, t_ref, early, me - 1).wait_recv()
                push(FIRST, 0, g, k, first, first, me - 1).wait_recv()
                push(FIRST, 0, g, k, first, first, me - 1).start()
                both = join(first[g, :, s], early[g, :, s])
                mine[g, :, s] = both
                every = join(both, t_ref[g, :, s])
                whole[g, :, s] = every

                @pl.when((z == 0) & (nz > 1))
                def _():
                    leave[g, :, s] = every[:states]
                    push(ENTER, 3, g, k, leave, enter, me + PLANE).start()
            loop(sub, up)

    def carry_stage(g):
        def merge(local, k):
            s = lanes(k)

            @pl.when(z > 0)
            def _():
                c_ref[g, :, s] = local[states:states + 1] * enter[g, :, s] + local[:states]

            @pl.when(z == 0)
            def _():
                c_ref[g, :, s] = local[:states]

        @pl.when(q == 0)
        def _():
            def body(k):
                s = lanes(k)

                @pl.when(z > 0)
                def _():
                    push(ENTER, 1, g, k, enter, enter, me + 1).wait_recv()
                    c_ref[g, :, s] = enter[g, :, s]

                @pl.when(z == 0)
                def _():
                    c_ref[g, :, s] = jnp.zeros((states, cw), F32)
            loop(sub, body)

        @pl.when(q == 1)
        def _():
            def body(k):
                @pl.when(z > 0)
                def _():
                    push(ENTER, 1, g, k, enter, enter, me - 1).wait_recv()
                    push(ENTER, 1, g, k, enter, enter, me - 1).start()
                merge(early[g, :, lanes(k)], k)
            loop(sub, body)

        @pl.when(q == 2)
        def _():
            def body(k):
                push(FIRST, 1, g, k, first, first, me + 1).wait_recv()

                @pl.when(z > 0)
                def _():
                    push(ENTER, 1, g, k, enter, enter, me + 1).wait_recv()
                merge(first[g, :, lanes(k)], k)
            loop(sub, body)

        @pl.when(q == 3)
        def _():
            def body(k):
                s = lanes(k)

                @pl.when(z > 0)
                def _():
                    push(ENTER, 1, g, k, enter, enter, me - 1).wait_recv()

                    @pl.when(z < nz - 1)
                    def _():
                        leave[g, :, s] = (
                            whole[g, states:states + 1, s] * enter[g, :, s] + whole[g, :states, s])
                        push(ENTER, 3, g, k, leave, enter, me + PLANE).start()

                    push(ENTER, 2, g, k, enter, enter, me - 2).start()
                    push(ENTER, 1, g, k, enter, enter, me - 1).start()
                merge(mine[g, :, s], k)
            loop(sub, body)

    def settle(g):
        def one(k):
            @pl.when((q == 0) | (q == 2))
            def _():
                push(EARLY, 0, g, k, t_ref, early, me + 1).wait_send()

            @pl.when(q == 1)
            def _():
                push(FIRST, 0, g, k, whole, first, me + 2).wait_send()

                @pl.when(z > 0)
                def _():
                    push(ENTER, 1, g, k, enter, enter, me - 1).wait_send()

            @pl.when(q == 3)
            def _():
                push(FIRST, 0, g, k, first, first, me - 1).wait_send()

                @pl.when(z < nz - 1)
                def _():
                    push(ENTER, 3, g, k, leave, enter, me + PLANE).wait_send()

                @pl.when(z > 0)
                def _():
                    push(ENTER, 2, g, k, enter, enter, me - 2).wait_send()
                    push(ENTER, 1, g, k, enter, enter, me - 1).wait_send()
        loop(sub, one)

    for part in few[2:]:
        part.wait()
    starts = starts_of(sizes_ref)
    rate_all = jnp.concatenate(
        [rate_ref[...], jnp.zeros((1, LANES - head_count), F32)], axis=1)
    rate_all = jnp.broadcast_to(-jnp.exp(rate_all), (8, LANES))

    def rows_of(b):
        return slice(b * BLOCK // slot, (b + 1) * BLOCK // slot)

    def y_of(g, b, lo, hi):
        return yr[g, rows_of(b), :, lo:hi].reshape(BLOCK, hi - lo)

    def states_stage(g):
        rate = group_lanes(rate_all, g, heads)[0:1]
        total = None
        for b in range(blocks):
            lo = b * BLOCK
            head = base + lo
            last = head + BLOCK - 1
            dt = dr[rows_of(b)].reshape(BLOCK, LANES).astype(F32)
            dt = group_lanes(dt, g, heads)
            cum = decay_of(dt, rate)
            cums[lo:lo + BLOCK, :] = cum
            dts[lo:lo + BLOCK, :] = dt
            end = cum[BLOCK - 1:BLOCK, :]
            pos = head + lax.broadcasted_iota(jnp.int32, (BLOCK, LANES), 0)
            last_seg = jnp.int32(0)
            cut = jnp.int32(0)
            for at in starts:
                last_seg = last_seg + (last >= at).astype(jnp.int32)
                cut = cut + ((at >= head) & (at <= last)).astype(jnp.int32)
            same = segment_of(pos, starts) == last_seg
            into = jnp.where(same, jnp.exp(end - cum), 0.0) * dt
            weighted = (y_of(g, b, 0, wx).astype(F32) * spread(into, heads, width)).astype(BF16)
            maps_t = y_of(g, b, wx, wx + wm).astype(F32).T
            in_map = maps_t[:states].astype(BF16)
            block_total = jnp.dot(in_map, weighted, preferred_element_type=F32)
            keep_h = jnp.where(cut == 0, jnp.exp(end), 0.0)
            keep = spread(jnp.broadcast_to(keep_h, (8, LANES)), heads, width)
            if total is None:
                total, gain = block_total, keep
            else:
                total = keep[0:1] * total + block_total
                gain = gain * keep
            if b < blocks - 1:
                t0_ref[g, b, :states, :] = block_total
                t0_ref[g, b, states:, :] = keep
        t_ref[g, :states, :] = total
        t_ref[g, states:, :] = gain

    def inner_stage(g):
        for b in range(blocks):
            lo = b * BLOCK
            head = base + lo
            cum = cums[lo:lo + BLOCK, :]
            cum_t = cum.T
            dt_t = dts[lo:lo + BLOCK, :].T
            pos_i = head + lax.broadcasted_iota(jnp.int32, (BLOCK, BLOCK), 0)
            pos_j = head + lax.broadcasted_iota(jnp.int32, (BLOCK, BLOCK), 1)
            allowed = (pos_i >= pos_j) & (segment_of(pos_i, starts) == segment_of(pos_j, starts))
            row_pos = head + lax.broadcasted_iota(jnp.int32, (1, BLOCK), 1)
            cut = jnp.zeros((1, BLOCK), jnp.int32)
            for at in starts:
                cut = cut + ((row_pos >= at) & (at >= head)).astype(jnp.int32)
            opens[g, b] = jnp.where(cut == 0, jnp.exp(cum_t[:heads]), 0.0)
            in_map = y_of(g, b, wx, wx + states)
            out_map = y_of(g, b, wx + states, wx + wm)
            gram = dot_nt(out_map, in_map)
            x_fm = y_of(g, b, 0, wx).T
            for h in range(heads):
                gap = jnp.broadcast_to(cum[:, h:h + 1], (BLOCK, BLOCK)) - cum_t[h:h + 1]
                mask = jnp.exp(jnp.where(allowed, gap, -jnp.inf))
                mixing = (gram * (mask * dt_t[h:h + 1])).astype(BF16)
                r = slice(h * width, (h + 1) * width)
                xh = x_fm[r]
                acc[g, r, lo:lo + BLOCK] = (
                    dot_nt(xh, mixing) + skip_ref[g * heads + h] * xh.astype(F32))

    def store_out(g):
        return pltpu.make_async_copy(
            obuf.at[g], o_hbm.at[pl.ds(pl.multiple_of(g * wx, LANES), wx)], out_sem.at[g])

    def output_stage(g):
        carry = c_ref[g]
        for b in range(blocks):
            lo = b * BLOCK
            out_map = y_of(g, b, wx + states, wx + wm)
            carried = dot_nt(carry.astype(BF16).T, out_map)
            for h in range(heads):
                r = slice(h * width, (h + 1) * width)
                obuf[g, r, lo:lo + BLOCK] = (
                    acc[g, r, lo:lo + BLOCK] + carried[r] * opens[g, b, h:h + 1]).astype(BF16)
            if b < blocks - 1:
                carry = t0_ref[g, b, states:states + 1, :] * carry + t0_ref[g, b, :states, :]
        store_out(g).start()

    loop(n, lambda off: send_d(off).wait_recv(), low=1)
    keep_d().wait()

    final = z == nz - 1
    ahead = (z < nz // 2) & jnp.logical_not(final)

    def settle_group(g):
        carry_stage(g)
        output_stage(g)

    def turn(g):
        @pl.when(ahead & (g == G - 1))
        def _():
            loop(G - 1, settle_group)

        loop(n, lambda off: send_y(g, off).wait_recv(), low=1)
        keep_y(g).wait()
        states_stage(g)
        open_stage(g)

        @pl.when(g == G - 1)
        def _():
            local_stage(g)

            @pl.when(jnp.logical_not(final))
            def _():
                loop(G - 1, settle_group, low=jnp.where(ahead, G - 1, 0))
                carry_stage(G - 1)

        inner_stage(g)

        @pl.when(g < G - 1)
        def _():
            local_stage(g)

    loop(G, turn)

    def wrap(g):
        @pl.when(final)
        def _():
            carry_stage(g)
        output_stage(g)

    loop(G, wrap, low=jnp.where(final, 0, G - 1))
    loop(n, lambda off: send_d(off).wait_send(), low=1)

    def close(g):
        loop(n, lambda off: send_y(g, off).wait_send(), low=1)
        settle(g)
        store_out(g).wait()

    loop(G, close)


def per_device(n, inputs, projections, step_sizes, log_rates, skip_gain, packing, prompt_sizes):
    tok = inputs.shape[1]
    head_count = log_rates.shape[0]
    heads = head_count // G
    states = projections.shape[0] // (2 * G)
    width = inputs.shape[0] // head_count
    wx = heads * width
    wm = 2 * states
    slot = tok // n
    blocks = tok // BLOCK
    rows = states + 8
    sub = 4
    hbm = pl.BlockSpec(memory_space=pltpu.HBM)
    dma = pltpu.SemaphoreType.DMA
    return pl.pallas_call(
        functools.partial(fused_kernel, n, heads, width, states, sub),
        in_specs=[hbm] * 7,
        out_specs=pl.BlockSpec(memory_space=pl.ANY),
        out_shape=jax.ShapeDtypeStruct((G * wx, tok), BF16),
        scratch_shapes=[
            pltpu.SMEM(prompt_sizes.shape, jnp.int32),
            pltpu.SMEM(skip_gain.shape, F32),
            pltpu.VMEM((1, head_count), F32),
            pltpu.VMEM((1, tok), jnp.int32),
            pltpu.VMEM((head_count, tok), BF16),
            pltpu.VMEM((G, wx, tok), BF16),
            pltpu.VMEM((G, wm, tok), BF16),
            pltpu.VMEM((tok, tok), BF16),
            pltpu.VMEM((G, n, slot, wx + wm), BF16),
            pltpu.VMEM((G, n, slot, wx + wm), BF16),
            pltpu.VMEM((n, slot, LANES), BF16),
            pltpu.VMEM((n, slot, LANES), BF16),
            pltpu.VMEM((tok, LANES), F32),
            pltpu.VMEM((tok, LANES), F32),
            pltpu.VMEM((G, wx, tok), F32),
            pltpu.VMEM((G, blocks, heads, BLOCK), F32),
            pltpu.VMEM((G, wx, tok), BF16),
            pltpu.VMEM((G, rows, wx), F32),
            pltpu.VMEM((G, blocks - 1, rows, wx), F32),
            pltpu.VMEM((G, rows, wx), F32),
            pltpu.VMEM((G, rows, wx), F32),
            pltpu.VMEM((G, rows, wx), F32),
            pltpu.VMEM((G, rows, wx), F32),
            pltpu.VMEM((G, states, wx), F32),
            pltpu.VMEM((G, states, wx), F32),
            pltpu.VMEM((G, states, wx), F32),
            dma((2, G)),
            dma((5,)),
            dma((G,)),
            dma((G,)),
            dma((1,)),
            dma((G, n)),
            dma((G, n)),
            dma((n,)),
            dma((n,)),
            dma((4, G, sub)),
            dma((3, G, sub)),
        ],
        compiler_params=pltpu.CompilerParams(
            collective_id=0, has_side_effects=True, vmem_limit_bytes=VLIM),
        name="prefill",
    )(*[pltpu.with_memory_space_constraint(part, pltpu.HBM) for part in (
        prompt_sizes, skip_gain, log_rates.reshape(1, head_count), packing,
        inputs, projections, step_sizes)])


def solution(mesh):
    in_specs = (
        P(None, ("groups", "ctx")),
        P(None, ("groups", "ctx")),
        P(None, ("groups", "ctx")),
        P(),
        P(),
        P(("groups", "ctx"), None),
        P("groups"),
    )
    out_specs = P(None, ("groups", "ctx"))
    return jax.shard_map(
        functools.partial(per_device, mesh.shape["ctx"]),
        mesh=mesh, in_specs=in_specs, out_specs=out_specs, check_vma=False,
    )
```
